32 devices in a mesh: wide: 8 (over y, x, core), narrow: 4 (over z).
Axes of the slice: x: 2, y: 2, z: 4, core: 2. Of those that a mesh axis runs over, the one named last changes fastest.
Arguments:
- hidden: bfloat16 [8, 256, 2048], P('wide', None, 'narrow'), may hold values from -6 to 6
- norm_gain: bfloat16 [2, 2048], replicated, may hold values from 0.25 to 1.75
- w_qkv: bfloat16 [2048, 3, 2048], P(None, None, 'narrow'), may hold values from -1 to 1
- qk_gain: float32 [2, 2048], P(None, 'narrow'), may hold values from 0.25 to 32
- w_out: bfloat16 [2048, 2048], P('narrow'), may hold values from -0.125 to 0.125
- cache: bfloat16 [2, 8, 2048, 2048], P(None, 'wide', None, 'narrow'), may hold values from -6 to 6
- lengths: int32 [8], replicated, may hold values from 1 to 2048, 8192 in all
- placing: int32 [8], replicated, may hold values from 0 to 7, each once
- routes: int32 [8, 256, 8], P('wide'), may hold values from 0 to 15, all different within a row; in each aligned block of 256 rows (0 to 255, 256 to 511, ..., all dimensions but the last counted through in order) at most 192 rows name the same one
- gate_w: float32 [8, 256, 8], P('wide'), may hold values from 0.02 to 0.3
- w_gu: bfloat16 [16, 2048, 2, 1024], P('wide', None, None, 'narrow'), may hold values from -0.125 to 0.125
- w_down: bfloat16 [16, 1024, 2048], P('wide', 'narrow'), may hold values from -0.1875 to 0.1875
Outputs:
- result: bfloat16 [8, 256, 2048], P('wide', None, 'narrow')
- new_cache: bfloat16 [2, 8, 256, 2048], P(None, 'wide', None, 'narrow')
The draws below stay inside these ranges and needn't reach their ends.
Inputs may be any that keep to these rules, and one draw needn't show every extreme that they name: `routes`: each token names 8 different experts; among the 256 tokens of one request no expert is named more than 192 times. `lengths`: some request has 2048 cached positions. Slot s holds request placing[s]; every request is held once.
All inputs are finite; a program needn't handle non-finite values.
Results may differ from the reference program's by a relative error of at most 0.013.
Values may be sent and summed in bfloat16 or wider, within the bound.
A program may use at most 128 MiB of HBM per device.

```python
import math
import jax
import jax.numpy as jnp
import numpy as np
from jax import lax

D = 2048
H = 16
HD = 128
FF = 1024
TOPK = 8
EXPERTS = 16
SPAN = 256
CACHE = 2048
REQS = 8
CAP = 192
N_NARROW = 4


def draw_hidden(key, part):
    inner = jax.random.fold_in(key, 11)
    values = jax.random.truncated_normal(inner, -6.0, 6.0, (REQS, SPAN, D), jnp.float32)
    return values.astype(jnp.bfloat16)


def draw_w_qkv(key, part):
    inner = jax.random.fold_in(key, 17)
    values = jax.random.truncated_normal(inner, -6.0, 6.0, (D, 3, H * HD), jnp.float32) * D ** (-0.5)
    return values.astype(jnp.bfloat16)


def draw_qk_gain(key, part):
    inner = jax.random.fold_in(key, 13)
    values = 1.0 + 0.15 * jax.random.truncated_normal(inner, -4.0, 4.0, (2, H * HD), jnp.float32)
    return values.astype(jnp.float32)


def shard_levels(key, shape, cuts, least, largest):
    gain = 1.0
    for axis_at, blocks in cuts:
        steps = jax.random.uniform(jax.random.fold_in(jax.random.fold_in(key, 6), axis_at), (blocks,), jnp.float32, least / len(cuts), largest / len(cuts))
        gain = gain * jnp.repeat(jnp.exp(steps), shape[axis_at] // blocks).reshape((-1,) + (1,) * (len(shape) - 1 - axis_at))
    return gain


def split_up(count, total, limit, lean):
    loads = [(1 << 20) // math.isqrt(standing ** lean) + 1 for standing in range(2, count + 1)]
    surplus, given = total - limit - (count - 1), [1] * (count - 1)
    while surplus > 0:
        free = [i for i in range(count - 1) if given[i] < limit]
        pool, left = sum([loads[i] for i in free]), surplus
        for i in free:
            extra = min(limit - given[i], max(1, left * loads[i] // pool), surplus)
            given[i] = given[i] + extra
            surplus = surplus - extra
    return np.array([limit] + given)


def uneven(own_key, amount, total, reach, slope):
    if amount == 2:
        one = jax.random.randint(own_key, (), max(1, total - reach), min(reach, total - 1) + 1)
        return jnp.stack([one, total - one])
    sizes = jnp.asarray(split_up(amount, total, reach, slope), jnp.int32)
    pairs = (amount - 1) // 2
    source_of, receiver = sizes[1:1 + 2 * pairs:2], sizes[2:2 + 2 * pairs:2]
    margin = jnp.minimum(source_of - 1, reach - receiver)
    shifted = jax.random.randint(jax.random.fold_in(own_key, 1), (pairs,), 0, 1 << 20) % (margin + 1)
    sizes = sizes.at[1:1 + 2 * pairs:2].set(source_of - shifted).at[2:2 + 2 * pairs:2].set(receiver + shifted)
    return sizes[jax.random.permutation(jax.random.fold_in(own_key, 2), amount)]


def shared_out(rng, own, number, rows, number_of, top, limit, skew):
    sequence = jax.random.permutation(rng, number_of)
    crowded, usual = portions_of(number_of, rows * top, limit, skew, True), portions_of(number_of, rows * top, limit, skew, False)
    places = jnp.arange(number_of)

    def named(sizes, turn):
        used = int((sizes > 0).sum())
        fixed = max(1, used // 4)
        passed = fixed + (places - fixed + turn * (used - fixed)) % max(1, number_of - fixed)
        return jnp.zeros((number_of,), jnp.int32).at[sequence[jnp.where(places < fixed, places, passed)]].set(jnp.asarray(sizes, jnp.int32))

    sizes = jnp.where(number % 4 == 0, named(crowded, number // 4), named(usual, number - number // 4 - 1))
    mixed = jax.random.permutation(jax.random.fold_in(own, 3), number_of)
    source_of, receiver = mixed[0:number_of // 2 * 2:2], mixed[1:number_of // 2 * 2:2]
    margin = jnp.minimum(sizes[source_of] - 1, limit - sizes[receiver]) // 2
    margin = jnp.where((source_of == sequence[0]) | (receiver == sequence[0]) | (sizes[receiver] == 0), 0, jnp.maximum(margin, 0))
    passed = jax.random.randint(jax.random.fold_in(own, 4), (number_of // 2,), 0, 1 << 20) % (margin + 1)
    sizes = sizes.at[source_of].add(-passed).at[receiver].add(passed)
    items = jnp.searchsorted(jnp.cumsum(sizes), jnp.arange(rows * top), side="right").astype(jnp.int32)
    listing = items.reshape(top, rows).T
    listing = listing[jax.random.permutation(jax.random.fold_in(own, 1), rows)]
    turn = jax.random.randint(jax.random.fold_in(own, 2), (rows, 1), 0, top)
    return jnp.take_along_axis(listing, (jnp.arange(top)[None, :] + turn) % top, axis=1)


def portions_of(amount, total, most, skew, full):
    portions = [(1 << 20) // math.isqrt(standing ** skew) + 1 for standing in range(1, amount + 1)]
    largest = most if full else min(most, max(-(-total // amount), total * portions[0] // sum(portions)))
    least = 1 if total - largest >= amount - 1 else 0
    given, surplus = [largest] + [least] * (amount - 1), total - largest - least * (amount - 1)
    while surplus > 0:
        free = [i for i in range(1, amount) if given[i] < largest] or [i for i in range(1, amount) if given[i] < most]
        pool, budget = sum([portions[i] for i in free]), surplus
        for i in free:
            addition = min(most - given[i], max(1, budget * portions[i] // pool), surplus)
            given[i] = given[i] + addition
            surplus = surplus - addition
    return np.array(given)


def scatter_about(key, extent, spread, bound, shards=(), held_as=jnp.bfloat16):
    values = jax.random.normal(key, extent, jnp.float32) * spread
    if len(shards) > 0:
        values = shard_levels(key, extent, shards, -0.22, 0.18) * values
    return jnp.clip(values, min=-bound, max=bound).astype(held_as)


def setup_inputs(seed: int = 0) -> dict:
    keys = jax.random.split(jax.random.key(seed), 13)
    hidden = draw_hidden(jax.random.fold_in(keys[12], 71), 0)
    norm_gain = jnp.clip(1.0 + 0.15 * jax.random.normal(keys[1], (2, D), jnp.float32), 0.25, 1.75).astype(jnp.bfloat16)
    w_qkv = draw_w_qkv(jax.random.fold_in(keys[12], 71), 0)
    qk_gain = draw_qk_gain(jax.random.fold_in(keys[12], 71), 0)
    w_out = scatter_about(keys[4], (H * HD, D), (H * HD) ** -0.5, 0.125, ((0, 4),))
    cache = scatter_about(keys[5], (2, REQS, CACHE, H * HD), 1.0, 6.0, ((1, 8), (3, 4)))
    lengths = uneven(keys[6], REQS, REQS * CACHE // 2, CACHE, 1).astype(jnp.int32)
    placing = jax.random.permutation(keys[7], REQS).astype(jnp.int32)
    routes_keys = jax.random.split(jax.random.fold_in(keys[8], 1), REQS * SPAN // SPAN)
    routes_turns = jax.random.permutation(jax.random.fold_in(keys[8], 3), REQS * SPAN // SPAN)
    routes = jax.vmap(lambda own, number: shared_out(jax.random.fold_in(keys[8], 2), own, number, SPAN, EXPERTS, TOPK, CAP, 1))(routes_keys, routes_turns).reshape((REQS, SPAN, TOPK))
    gate_w = jnp.clip(jnp.exp(math.log(0.3) - 2.7080503 * jax.random.uniform(keys[9], (REQS, SPAN, TOPK), jnp.float32) ** shard_levels(keys[9], (REQS, SPAN, TOPK), ((0, 8),), -0.2, 0.2)), 0.02, 0.3)
    w_gu = scatter_about(keys[10], (EXPERTS, D, 2, FF), D ** -0.5, 0.125, ((0, 8), (3, 4)))
    w_down = scatter_about(keys[11], (EXPERTS, FF, D), FF ** -0.5, 0.1875, ((0, 8), (1, 4)))
    return dict(hidden=hidden, norm_gain=norm_gain, w_qkv=w_qkv, qk_gain=qk_gain, w_out=w_out, cache=cache, lengths=lengths, placing=placing, routes=routes, gate_w=gate_w, w_gu=w_gu, w_down=w_down)


def normalize(values, gain_row):
    values = values.astype(jnp.float32)
    return values * lax.rsqrt(lax.optimization_barrier(jnp.mean(values * values, axis=-1, keepdims=True)) + 1e-05) * gain_row.astype(jnp.float32)

def rotary(values, positions):
    half_dim = values.shape[-1] // 2
    frequency = 10000.0 ** (-(jnp.arange(half_dim, dtype=jnp.float32) * (2.0 / values.shape[-1])))
    angle = positions[:, None] * frequency[None, :]
    cosine = jnp.cos(angle)[:, None, :]
    sine_part = jnp.sin(angle)[:, None, :]
    first_half = values[..., :half_dim]
    second_half = values[..., half_dim:]
    return jnp.concatenate([first_half * cosine - second_half * sine_part, second_half * cosine + first_half * sine_part], axis=-1)

def attend(pieces, norm_gain, w_qkv, qk_gain, w_out):
    tokens, keys_old, values_old, length = pieces
    span_len = tokens.shape[0]
    features = H * HD
    normed = normalize(tokens, norm_gain[0]).astype(jnp.bfloat16)
    projected = jnp.dot(normed, w_qkv.reshape(D, 3 * features), preferred_element_type=jnp.float32)
    queries = normalize(projected[:, :features], qk_gain[0])
    keys_new = normalize(projected[:, features:2 * features], qk_gain[1])
    values_new = projected[:, 2 * features:]
    positions = length.astype(jnp.float32) + jnp.arange(span_len, dtype=jnp.float32)
    queries = rotary(queries.reshape(span_len, H, HD), positions).astype(jnp.bfloat16)
    keys_new = rotary(keys_new.reshape(span_len, H, HD), positions).astype(jnp.bfloat16)
    values_new = values_new.reshape(span_len, H, HD).astype(jnp.bfloat16)
    all_keys = jnp.concatenate([keys_old.reshape(CACHE, H, HD), keys_new], 0)
    all_values = jnp.concatenate([values_old.reshape(CACHE, H, HD), values_new], 0)
    scores = jnp.einsum('thd,jhd->htj', queries.astype(jnp.float32), all_keys.astype(jnp.float32)) * HD ** (-0.5)
    key_index = jnp.arange(CACHE + span_len, dtype=jnp.int32)[None, :]
    query_index = jnp.arange(span_len, dtype=jnp.int32)[:, None]
    allowed = jnp.where(key_index < CACHE, key_index < length, key_index - CACHE <= query_index)
    scores = jnp.where(allowed[None], scores, -1e+30)
    highest = lax.optimization_barrier(jnp.max(scores, axis=-1, keepdims=True))
    exponent = jnp.exp(scores - highest)
    weights = exponent.astype(jnp.bfloat16)
    denominator = lax.optimization_barrier(jnp.sum(exponent, axis=-1))
    summed = jnp.einsum('htj,jhd->thd', weights.astype(jnp.float32), all_values.astype(jnp.float32))
    heads_out = (summed / jnp.transpose(denominator)[:, :, None]).astype(jnp.bfloat16).reshape(span_len, features)
    attention = jnp.dot(heads_out, w_out, preferred_element_type=jnp.float32)
    after = (tokens.astype(jnp.float32) + attention).astype(jnp.bfloat16)
    fresh = jnp.stack([keys_new.reshape(span_len, features), values_new.reshape(span_len, features)])
    return (after, fresh)

def reference(hidden, norm_gain, w_qkv, qk_gain, w_out, cache, lengths, placing, routes, gate_w, w_gu, w_down):
    slot_length = lengths[placing]
    after, fresh = lax.map(lambda pieces: attend(pieces, norm_gain, w_qkv, qk_gain, w_out), (hidden, cache[0], cache[1], slot_length))
    new_cache = jnp.transpose(fresh, (1, 0, 2, 3))
    requests = hidden.shape[0]
    span_len = hidden.shape[1]
    experts = w_gu.shape[0]
    routed = normalize(after, norm_gain[1]).astype(jnp.bfloat16).reshape(requests * span_len, D)
    padded = jnp.concatenate([routed, jnp.zeros((1, D), jnp.bfloat16)], 0)

    def ranks(block_routes):
        flat_routes = block_routes.reshape(-1)
        onehot = (flat_routes[:, None] == jnp.arange(experts, dtype=jnp.int32)[None, :]).astype(jnp.int32)
        return lax.optimization_barrier(jnp.sum((jnp.cumsum(onehot, 0) - onehot) * onehot, 1))
    slot_rank = jax.vmap(ranks)(routes)
    flat_routes = routes.reshape(requests, span_len * TOPK)
    owner_slot = jnp.arange(requests, dtype=jnp.int32)[:, None]
    target = flat_routes * (requests * CAP) + owner_slot * CAP + slot_rank
    token_row = owner_slot * span_len + (jnp.arange(span_len * TOPK, dtype=jnp.int32) // TOPK)[None, :]
    source_row = jnp.full((experts * requests * CAP,), requests * span_len, jnp.int32).at[target.reshape(-1)].set(token_row.reshape(-1))
    gate_table = jnp.zeros((experts * requests * CAP,), jnp.float32).at[target.reshape(-1)].set(gate_w.reshape(-1).astype(jnp.float32))
    source_row = source_row.reshape(experts, requests * CAP)
    gate_table = gate_table.reshape(experts, requests * CAP)
    groups = N_NARROW
    group_width = FF // groups

    def expert_step(accum, item):
        gate_up, down_rows, rows_used, gate_scale = item
        inputs = padded[rows_used].astype(jnp.float32)
        projected = jnp.dot(inputs, gate_up.reshape(D, 2 * FF).astype(jnp.float32))
        activated = (jax.nn.silu(projected[:, :FF]) * projected[:, FF:]).astype(jnp.bfloat16)
        parts = jnp.einsum('rnf,nfd->nrd', activated.reshape(-1, groups, group_width).astype(jnp.float32), down_rows.reshape(groups, group_width, D).astype(jnp.float32)).astype(jnp.bfloat16)
        expert_sum = lax.optimization_barrier(jnp.sum(parts.astype(jnp.float32), 0))
        return (accum.at[rows_used].add(gate_scale[:, None] * expert_sum), None)
    accum, _ = lax.scan(expert_step, jnp.zeros((requests * span_len + 1, D), jnp.float32), (w_gu, w_down, source_row, gate_table))
    result = (after.reshape(requests * span_len, D).astype(jnp.float32) + accum[:requests * span_len]).astype(jnp.bfloat16)
    return (result.reshape(requests, span_len, D), new_cache)
```

```python
import jax
import jax.numpy as jnp
from jax import lax
from jax.sharding import PartitionSpec as P

HD = 128


def normalize(values, gain_row):
    values = values.astype(jnp.float32)
    return (
        values
        * lax.rsqrt(jnp.mean(values * values, axis=-1, keepdims=True) + 1e-05)
        * gain_row.astype(jnp.float32)
    )


def rotary(values, positions):
    half_dim = values.shape[-1] // 2
    frequency = 10000.0 ** (-(jnp.arange(half_dim, dtype=jnp.float32) * (2.0 / values.shape[-1])))
    angle = positions[:, None] * frequency[None, :]
    cosine = jnp.cos(angle)[:, None, :]
    sine_part = jnp.sin(angle)[:, None, :]
    first_half = values[..., :half_dim]
    second_half = values[..., half_dim:]
    return jnp.concatenate(
        [
            first_half * cosine - second_half * sine_part,
            second_half * cosine + first_half * sine_part,
        ],
        axis=-1,
    )


def per_device(
    hidden, norm_gain, w_qkv, qk_gain, w_out, cache, lengths, placing, routes, gate_w, w_gu, w_down
):
    narrow = lax.axis_size("narrow")
    wide_size = lax.axis_size("wide")
    column = lax.axis_index("narrow")
    position = lax.axis_index("wide")
    span_len = hidden.shape[1]
    share_cols = hidden.shape[2]
    full_width = share_cols * narrow
    tokens = lax.all_gather(hidden[0], "narrow", axis=1, tiled=True)
    normed = normalize(tokens, norm_gain[0]).astype(jnp.bfloat16)
    local_cols = w_qkv.shape[2]
    projected = jnp.dot(
        normed, w_qkv.reshape(full_width, 3 * local_cols), preferred_element_type=jnp.float32
    )
    queries = projected[:, :local_cols]
    keys_new = projected[:, local_cols : 2 * local_cols]
    values_new = projected[:, 2 * local_cols :]
    squares = lax.psum((jnp.sum(queries * queries, -1), jnp.sum(keys_new * keys_new, -1)), "narrow")
    features = local_cols * narrow
    queries = queries * lax.rsqrt(squares[0][:, None] / features + 1e-05) * qk_gain[0]
    keys_new = keys_new * lax.rsqrt(squares[1][:, None] / features + 1e-05) * qk_gain[1]
    head_count = local_cols // HD
    length = lengths[placing[position]]
    positions = length.astype(jnp.float32) + jnp.arange(span_len, dtype=jnp.float32)
    queries = rotary(queries.reshape(span_len, head_count, HD), positions).astype(jnp.bfloat16)
    keys_new = rotary(keys_new.reshape(span_len, head_count, HD), positions).astype(jnp.bfloat16)
    values_new = values_new.reshape(span_len, head_count, HD).astype(jnp.bfloat16)
    stored = cache.shape[2]
    all_keys = jnp.concatenate([cache[0, 0].reshape(stored, head_count, HD), keys_new], 0)
    all_values = jnp.concatenate([cache[1, 0].reshape(stored, head_count, HD), values_new], 0)
    scores = jnp.einsum(
        "thd,jhd->htj", queries, all_keys, preferred_element_type=jnp.float32
    ) * HD ** (-0.5)
    key_index = jnp.arange(stored + span_len, dtype=jnp.int32)[None, :]
    query_index = jnp.arange(span_len, dtype=jnp.int32)[:, None]
    allowed = jnp.where(key_index < stored, key_index < length, key_index - stored <= query_index)
    scores = jnp.where(allowed[None], scores, -1e30)
    highest = jnp.max(scores, axis=-1, keepdims=True)
    exponent = jnp.exp(scores - highest)
    weights = exponent.astype(jnp.bfloat16)
    denominator = jnp.sum(exponent, axis=-1)
    summed = jnp.einsum("htj,jhd->thd", weights, all_values, preferred_element_type=jnp.float32)
    heads_out = (
        (summed / jnp.transpose(denominator)[:, :, None])
        .astype(jnp.bfloat16)
        .reshape(span_len, local_cols)
    )
    partial_out = jnp.dot(heads_out, w_out, preferred_element_type=jnp.float32)
    rows = span_len // narrow
    attention = lax.psum_scatter(
        partial_out.astype(jnp.bfloat16), "narrow", scatter_dimension=0, tiled=True
    ).astype(jnp.float32)
    own_rows = lax.dynamic_slice_in_dim(tokens, column * rows, rows, 0)
    after_rows = (own_rows.astype(jnp.float32) + attention).astype(jnp.bfloat16)
    after_all = lax.all_gather(after_rows, ("wide", "narrow"), axis=0, tiled=True)
    after_own = lax.dynamic_slice(
        after_all, (position * span_len, column * share_cols), (span_len, share_cols)
    )
    routed = normalize(after_all, norm_gain[1]).astype(jnp.bfloat16)
    held_experts = w_gu.shape[0]
    inner_cols = w_gu.shape[3]
    experts = held_experts * wide_size
    named = routes[0][:, :, None] == jnp.arange(experts, dtype=jnp.int32)[None, None, :]
    table = jnp.sum(jnp.where(named, gate_w[0][:, :, None], 0.0), axis=1)
    table = lax.all_gather(table, "wide", axis=0, tiled=True)
    scale = lax.dynamic_slice_in_dim(table, position * held_experts, held_experts, 1)
    pieces = []
    for j in range(held_experts):
        gate_up = jnp.dot(
            routed,
            w_gu[j].reshape(full_width, 2 * inner_cols),
            preferred_element_type=jnp.float32,
        )
        activated = jax.nn.silu(gate_up[:, :inner_cols]) * gate_up[:, inner_cols:]
        pieces.append((activated * scale[:, j : j + 1]).astype(jnp.bfloat16))
    weighted = jnp.concatenate(pieces, 1)
    combined = jnp.dot(
        weighted,
        w_down.reshape(held_experts * inner_cols, full_width),
        preferred_element_type=jnp.float32,
    ).astype(jnp.bfloat16)
    combined = lax.psum_scatter(combined, "wide", scatter_dimension=0, tiled=True)
    expert_out = lax.psum_scatter(
        combined, "narrow", scatter_dimension=1, tiled=True
    ).astype(jnp.float32)
    result = (after_own.astype(jnp.float32) + expert_out).astype(jnp.bfloat16)[None]
    fresh = jnp.stack(
        [keys_new.reshape(span_len, local_cols), values_new.reshape(span_len, local_cols)]
    )[:, None]
    return (result, fresh)


def solution(mesh):
    placed = (
        P("wide", None, "narrow"),
        P(),
        P(None, None, "narrow"),
        P(None, "narrow"),
        P("narrow", None),
        P(None, "wide", None, "narrow"),
        P(),
        P(),
        P("wide", None, None),
        P("wide", None, None),
        P("wide", None, None, "narrow"),
        P("wide", "narrow", None),
    )
    return jax.shard_map(
        per_device,
        mesh=mesh,
        in_specs=placed,
        out_specs=(P("wide", None, "narrow"), P(None, "wide", None, "narrow")),
        check_vma=False,
    )
```

```python
import jax
import jax.numpy as jnp
from jax import lax
from jax.experimental import pallas as pl
from jax.experimental.pallas import tpu as pltpu
from jax.sharding import PartitionSpec as P

HD = 128


def normalize(values, gain_row):
    values = values.astype(jnp.float32)
    return (
        values
        * lax.rsqrt(jnp.mean(values * values, axis=-1, keepdims=True) + 1e-05)
        * gain_row.astype(jnp.float32)
    )


def rotary(values, positions):
    half_dim = values.shape[-1] // 2
    frequency = 10000.0 ** (-(jnp.arange(half_dim, dtype=jnp.float32) * (2.0 / values.shape[-1])))
    angle = positions[:, None] * frequency[None, :]
    cosine = jnp.cos(angle)[:, None, :]
    sine_part = jnp.sin(angle)[:, None, :]
    first_half = values[..., :half_dim]
    second_half = values[..., half_dim:]
    return jnp.concatenate(
        [
            first_half * cosine - second_half * sine_part,
            second_half * cosine + first_half * sine_part,
        ],
        axis=-1,
    )


TAIL = 128
VMEM_LIMIT = 56 * 1024 * 1024


def places():
    w = lax.axis_index("wide")
    z = lax.axis_index("narrow")
    c = lax.rem(w, 2)
    dx = 2 - 4 * lax.rem(lax.div(w, 2), 2)
    dy = 4 - 8 * lax.div(w, 4)
    first = dx * (1 - c) + dy * c
    second = dy * (1 - c) + dx * c
    return w, z, 1 - 2 * c, first, second


def greet(w, z, sib, first, second):
    barrier = pltpu.get_barrier_semaphore()
    for step in (sib, first, second):
        pl.semaphore_signal(
            barrier, inc=1, device_id={"wide": w + step}, device_id_type=pl.DeviceIdType.MESH
        )
    for k in (1, 2, 3):
        pl.semaphore_signal(
            barrier,
            inc=1,
            device_id={"narrow": lax.rem(z + k, 4)},
            device_id_type=pl.DeviceIdType.MESH,
        )
    pl.semaphore_wait(barrier, 6)


def gather_kernel(rows_ref, gu_ref, out_ref, held, send, recv):
    w, z, sib, first, second = places()
    width = gu_ref.shape[1]
    inner = gu_ref.shape[2] // 2
    experts_held = gu_ref.shape[0]
    experts = experts_held * 8
    mine = (0, first, second, first + second)
    theirs = (sib, sib + second, sib + first, sib + first + second)
    slots = [w + step for step in mine + theirs]
    held[z, w] = rows_ref[...]
    greet(w, z, sib, first, second)
    started = []

    def piece(slot, k, role, device):
        ref = held.at[lax.rem(z + 4 - k, 4), slot]
        return pltpu.make_async_remote_copy(
            src_ref=ref,
            dst_ref=ref,
            send_sem=send.at[len(started)],
            recv_sem=recv.at[role, k],
            device_id=device,
            device_id_type=pl.DeviceIdType.MESH,
        )

    def push(slot, k, role, step):
        copy = piece(slot, k, role, {"wide": w + step})
        copy.start()
        started.append(copy)

    def arrive(role, k):
        ref = held.at[lax.rem(z + 4 - k, 4), slots[role]]
        pltpu.make_async_remote_copy(
            src_ref=ref,
            dst_ref=ref,
            send_sem=send.at[0],
            recv_sem=recv.at[role, k],
            device_id={"wide": w + sib},
            device_id_type=pl.DeviceIdType.MESH,
        ).wait_recv()

    def expert_rows(k):
        group = lax.rem(z + 4 - k, 4)

        def half(h, carry):
            rows = held.shape[2]
            values = held[group, pl.ds(h * 4, 4)]
            inputs = values[:, :, :width].reshape(4 * rows, width)
            tail = values[:, :, width:].reshape(4 * rows, TAIL).astype(jnp.float32)
            lane = lax.broadcasted_iota(jnp.int32, tail.shape, 1)
            for j in range(experts_held):
                e = w * experts_held + j
                hit = (lane == e) | (lane == e + experts) | (lane == e + 2 * experts)
                scale = jnp.sum(jnp.where(hit, tail, 0.0), axis=1, keepdims=True)
                both = jnp.dot(inputs, gu_ref[j], preferred_element_type=jnp.float32)
                gate = both[:, :inner]
                active = gate / (1.0 + jnp.exp(-gate)) * both[:, inner:] * scale
                out_ref[group, pl.ds(h * 4, 4), :, j * inner : (j + 1) * inner] = active.astype(
                    jnp.bfloat16
                ).reshape(4, rows, inner)
            return carry

        lax.fori_loop(0, 2, half, 0)

    for k in (1, 3, 2):
        ref = held.at[z, w]
        copy = pltpu.make_async_remote_copy(
            src_ref=ref,
            dst_ref=ref,
            send_sem=send.at[len(started)],
            recv_sem=recv.at[0, k],
            device_id={"narrow": lax.rem(z + k, 4)},
            device_id_type=pl.DeviceIdType.MESH,
        )
        copy.start()
        started.append(copy)
    order = (0, 1, 3, 2)
    for t in range(7):
        if t < 4:
            k = order[t]
            if k:
                arrive(0, k)
            push(w, k, 1, first)
            push(w, k, 2, second)
            push(w, k, 4, sib)
        if 1 <= t < 5:
            k = order[t - 1]
            arrive(1, k)
            push(slots[1], k, 3, second)
            push(slots[1], k, 5, sib)
            arrive(2, k)
            push(slots[2], k, 6, sib)
        if 2 <= t < 6:
            k = order[t - 2]
            arrive(3, k)
            push(slots[3], k, 7, sib)
        if 3 <= t:
            k = order[t - 3]
            for role in (4, 5, 6, 7):
                arrive(role, k)
            expert_rows(k)
    for copy in started:
        copy.wait_send()


def gather_experts(rows_in, gu):
    rows, padded = rows_in.shape
    held, _, both = gu.shape
    return pl.pallas_call(
        gather_kernel,
        out_shape=jax.ShapeDtypeStruct((4, 8, rows, held * both // 2), jnp.bfloat16),
        in_specs=[pl.BlockSpec(memory_space=pltpu.VMEM)] * 2,
        out_specs=pl.BlockSpec(memory_space=pltpu.VMEM),
        scratch_shapes=[
            pltpu.VMEM((4, 8, rows, padded), jnp.bfloat16),
            pltpu.SemaphoreType.DMA((31,)),
            pltpu.SemaphoreType.DMA((8, 4)),
        ],
        compiler_params=pltpu.CompilerParams(
            collective_id=0, has_side_effects=True, vmem_limit_bytes=VMEM_LIMIT
        ),
        name="gather_experts",
    )(rows_in, gu)


def reduce_kernel(
    weighted_ref,
    down_ref,
    after_ref,
    out_ref,
    sib_out,
    sib_in,
    first_out,
    first_keep,
    first_in,
    second_out,
    second_keep,
    second_in,
    z_out,
    z_in,
    after_in,
    total,
    send,
    recv,
):
    w, z, sib, first, second = places()
    span, cols = out_ref.shape
    rows = after_ref.shape[0]
    mine = (0, first, second, first + second)
    theirs = (sib, sib + second, sib + first, sib + first + second)
    greet(w, z, sib, first, second)
    started = []

    def push(src, dst, number, device):
        copy = pltpu.make_async_remote_copy(
            src_ref=src,
            dst_ref=dst,
            send_sem=send.at[number],
            recv_sem=recv.at[number],
            device_id=device,
            device_id_type=pl.DeviceIdType.MESH,
        )
        copy.start()
        started.append(copy)

    def arrive(dst, number):
        pltpu.make_async_remote_copy(
            src_ref=dst,
            dst_ref=dst,
            send_sem=send.at[number],
            recv_sem=recv.at[number],
            device_id={"wide": w + sib},
            device_id_type=pl.DeviceIdType.MESH,
        ).wait_recv()

    def columns(k):
        return pl.ds(pl.multiple_of(lax.rem(z + k, 4) * cols, cols), cols)

    def product(slot, k):
        values = weighted_ref[:, slot].reshape(span, weighted_ref.shape[3])
        return jnp.dot(values, down_ref[:, columns(k)], preferred_element_type=jnp.float32)

    for k in (1, 3, 2):
        push(
            after_ref.at[:, columns(k)],
            after_in.at[k],
            20 + k,
            {"narrow": lax.rem(z + k, 4)},
        )
    order = (2, 1, 3, 0)
    for t in range(7):
        if t < 4:
            k = order[t]
            for r in range(4):
                sib_out[k, r] = product(w + theirs[r], k).astype(jnp.bfloat16)
            push(sib_out.at[k], sib_in.at[k], k, {"wide": w + sib})
        if 1 <= t < 5:
            k = order[t - 1]
            arrive(sib_in.at[k], k)
            for spot, r in ((0, 1), (1, 3)):
                value = product(w + mine[r], k) + sib_in[k, r].astype(jnp.float32)
                first_out[k, spot] = value.astype(jnp.bfloat16)
            push(first_out.at[k], first_in.at[k], 4 + k, {"wide": w + first})
            for spot, r in ((0, 0), (1, 2)):
                first_keep[k, spot] = product(w + mine[r], k) + sib_in[k, r].astype(jnp.float32)
        if 2 <= t < 6:
            k = order[t - 2]
            arrive(first_in.at[k], 4 + k)
            second_out[k] = (first_keep[k, 1] + first_in[k, 1].astype(jnp.float32)).astype(
                jnp.bfloat16
            )
            push(second_out.at[k], second_in.at[k], 8 + k, {"wide": w + second})
            second_keep[k] = first_keep[k, 0] + first_in[k, 0].astype(jnp.float32)
        if 3 <= t:
            k = order[t - 3]
            arrive(second_in.at[k], 8 + k)
            value = second_keep[k] + second_in[k].astype(jnp.float32)
            if k:
                z_out[k] = value.astype(jnp.bfloat16)
                push(z_out.at[k], z_in.at[k], 12 + k, {"narrow": lax.rem(z + k, 4)})
            else:
                total[...] = value
    for k in (1, 2, 3):
        arrive(z_in.at[k], 12 + k)
        arrive(after_in.at[k], 20 + k)
    total[...] = total[...] + (
        z_in[1].astype(jnp.float32) + z_in[2].astype(jnp.float32) + z_in[3].astype(jnp.float32)
    )
    for k in range(4):
        block = pl.ds(pl.multiple_of(lax.rem(z + 4 - k, 4) * rows, rows), rows)
        own = after_in[k] if k else after_ref[:, columns(0)]
        out_ref[block, :] = (total[block, :] + own.astype(jnp.float32)).astype(jnp.bfloat16)
    for copy in started:
        copy.wait_send()


def reduce_experts(weighted, down, after_rows):
    rows, width = after_rows.shape
    span, cols = rows * 4, width // 4
    half = jnp.bfloat16
    return pl.pallas_call(
        reduce_kernel,
        out_shape=jax.ShapeDtypeStruct((span, cols), half),
        in_specs=[pl.BlockSpec(memory_space=pltpu.VMEM)] * 3,
        out_specs=pl.BlockSpec(memory_space=pltpu.VMEM),
        scratch_shapes=[
            pltpu.VMEM((4, 4, span, cols), half),
            pltpu.VMEM((4, 4, span, cols), half),
            pltpu.VMEM((4, 2, span, cols), half),
            pltpu.VMEM((4, 2, span, cols), jnp.float32),
            pltpu.VMEM((4, 2, span, cols), half),
            pltpu.VMEM((4, span, cols), half),
            pltpu.VMEM((4, span, cols), jnp.float32),
            pltpu.VMEM((4, span, cols), half),
            pltpu.VMEM((4, span, cols), half),
            pltpu.VMEM((4, span, cols), half),
            pltpu.VMEM((4, rows, cols), half),
            pltpu.VMEM((span, cols), jnp.float32),
            pltpu.SemaphoreType.DMA((24,)),
            pltpu.SemaphoreType.DMA((24,)),
        ],
        compiler_params=pltpu.CompilerParams(
            collective_id=1, has_side_effects=True, vmem_limit_bytes=VMEM_LIMIT
        ),
        name="reduce_experts",
    )(weighted, down, after_rows)


def router_table(routes, gate_w, experts):
    named = routes[:, :, None] == jnp.arange(experts, dtype=jnp.int32)[None, None, :]
    return jnp.sum(jnp.where(named, gate_w[:, :, None], 0.0), axis=1)


def in_three(values):
    high = values.astype(jnp.bfloat16)
    rest = values - high.astype(jnp.float32)
    middle = rest.astype(jnp.bfloat16)
    low = (rest - middle.astype(jnp.float32)).astype(jnp.bfloat16)
    return [high, middle, low]


def experts_by_copies(after_rows, gain, routes, gate_w, w_gu, w_down):
    rows, width = after_rows.shape
    held, _, _, inner = w_gu.shape
    experts = held * 8
    column = lax.axis_index("narrow")
    routed = normalize(after_rows, gain).astype(jnp.bfloat16)
    table = router_table(
        lax.dynamic_slice_in_dim(routes, column * rows, rows, 0),
        lax.dynamic_slice_in_dim(gate_w, column * rows, rows, 0),
        experts,
    )
    filler = jnp.zeros((rows, TAIL - 3 * experts), jnp.bfloat16)
    rows_in = jnp.concatenate([routed] + in_three(table) + [filler], 1)
    weighted = gather_experts(rows_in, w_gu.reshape(held, width, 2 * inner))
    return reduce_experts(weighted, w_down.reshape(held * inner, width), after_rows)


def experts_by_collectives(after_rows, gain, routes, gate_w, w_gu, w_down):
    position = lax.axis_index("wide")
    column = lax.axis_index("narrow")
    wide_size = lax.axis_size("wide")
    narrow = lax.axis_size("narrow")
    rows, full_width = after_rows.shape
    span_len, share_cols = rows * narrow, full_width // narrow
    after_all = lax.all_gather(after_rows, ("wide", "narrow"), axis=0, tiled=True)
    after_own = lax.dynamic_slice(
        after_all, (position * span_len, column * share_cols), (span_len, share_cols)
    )
    routed = normalize(after_all, gain).astype(jnp.bfloat16)
    held_experts = w_gu.shape[0]
    inner_cols = w_gu.shape[3]
    experts = held_experts * wide_size
    table = router_table(routes, gate_w, experts)
    table = lax.all_gather(table, "wide", axis=0, tiled=True)
    scale = lax.dynamic_slice_in_dim(table, position * held_experts, held_experts, 1)
    pieces = []
    for j in range(held_experts):
        gate_up = jnp.dot(
            routed,
            w_gu[j].reshape(full_width, 2 * inner_cols),
            preferred_element_type=jnp.float32,
        )
        activated = jax.nn.silu(gate_up[:, :inner_cols]) * gate_up[:, inner_cols:]
        pieces.append((activated * scale[:, j : j + 1]).astype(jnp.bfloat16))
    weighted = jnp.concatenate(pieces, 1)
    combined = jnp.dot(
        weighted,
        w_down.reshape(held_experts * inner_cols, full_width),
        preferred_element_type=jnp.float32,
    ).astype(jnp.bfloat16)
    combined = lax.psum_scatter(combined, "wide", scatter_dimension=0, tiled=True)
    expert_out = lax.psum_scatter(
        combined, "narrow", scatter_dimension=1, tiled=True
    ).astype(jnp.float32)
    return (after_own.astype(jnp.float32) + expert_out).astype(jnp.bfloat16)

def per_device(
    hidden, norm_gain, w_qkv, qk_gain, w_out, cache, lengths, placing, routes, gate_w, w_gu, w_down
):
    narrow = lax.axis_size("narrow")
    wide_size = lax.axis_size("wide")
    column = lax.axis_index("narrow")
    position = lax.axis_index("wide")
    span_len = hidden.shape[1]
    share_cols = hidden.shape[2]
    full_width = share_cols * narrow
    tokens = lax.all_gather(hidden[0], "narrow", axis=1, tiled=True)
    normed = normalize(tokens, norm_gain[0]).astype(jnp.bfloat16)
    local_cols = w_qkv.shape[2]
    projected = jnp.dot(
        normed, w_qkv.reshape(full_width, 3 * local_cols), preferred_element_type=jnp.float32
    )
    queries = projected[:, :local_cols]
    keys_new = projected[:, local_cols : 2 * local_cols]
    values_new = projected[:, 2 * local_cols :]
    squares = lax.psum((jnp.sum(queries * queries, -1), jnp.sum(keys_new * keys_new, -1)), "narrow")
    features = local_cols * narrow
    queries = queries * lax.rsqrt(squares[0][:, None] / features + 1e-05) * qk_gain[0]
    keys_new = keys_new * lax.rsqrt(squares[1][:, None] / features + 1e-05) * qk_gain[1]
    head_count = local_cols // HD
    length = lengths[placing[position]]
    positions = length.astype(jnp.float32) + jnp.arange(span_len, dtype=jnp.float32)
    queries = rotary(queries.reshape(span_len, head_count, HD), positions).astype(jnp.bfloat16)
    keys_new = rotary(keys_new.reshape(span_len, head_count, HD), positions).astype(jnp.bfloat16)
    values_new = values_new.reshape(span_len, head_count, HD).astype(jnp.bfloat16)
    stored = cache.shape[2]
    all_keys = jnp.concatenate([cache[0, 0].reshape(stored, head_count, HD), keys_new], 0)
    all_values = jnp.concatenate([cache[1, 0].reshape(stored, head_count, HD), values_new], 0)
    scores = jnp.einsum(
        "thd,jhd->htj", queries, all_keys, preferred_element_type=jnp.float32
    ) * HD ** (-0.5)
    key_index = jnp.arange(stored + span_len, dtype=jnp.int32)[None, :]
    query_index = jnp.arange(span_len, dtype=jnp.int32)[:, None]
    allowed = jnp.where(key_index < stored, key_index < length, key_index - stored <= query_index)
    scores = jnp.where(allowed[None], scores, -1e30)
    highest = jnp.max(scores, axis=-1, keepdims=True)
    exponent = jnp.exp(scores - highest)
    weights = exponent.astype(jnp.bfloat16)
    denominator = jnp.sum(exponent, axis=-1)
    summed = jnp.einsum("htj,jhd->thd", weights, all_values, preferred_element_type=jnp.float32)
    heads_out = (
        (summed / jnp.transpose(denominator)[:, :, None])
        .astype(jnp.bfloat16)
        .reshape(span_len, local_cols)
    )
    partial_out = jnp.dot(heads_out, w_out, preferred_element_type=jnp.float32)
    rows = span_len // narrow
    attention = lax.psum_scatter(
        partial_out.astype(jnp.bfloat16), "narrow", scatter_dimension=0, tiled=True
    ).astype(jnp.float32)
    own_rows = lax.dynamic_slice_in_dim(tokens, column * rows, rows, 0)
    after_rows = (own_rows.astype(jnp.float32) + attention).astype(jnp.bfloat16)
    by_copies = wide_size == 8 and narrow == 4 and w_gu.shape[0] * 24 <= TAIL
    experts_of = experts_by_copies if by_copies else experts_by_collectives
    result = experts_of(after_rows, norm_gain[1], routes[0], gate_w[0], w_gu, w_down)[None]
    fresh = jnp.stack(
        [keys_new.reshape(span_len, local_cols), values_new.reshape(span_len, local_cols)]
    )[:, None]
    return (result, fresh)


def solution(mesh):
    placed = (
        P("wide", None, "narrow"),
        P(),
        P(None, None, "narrow"),
        P(None, "narrow"),
        P("narrow", None),
        P(None, "wide", None, "narrow"),
        P(),
        P(),
        P("wide", None, None),
        P("wide", None, None),
        P("wide", None, None, "narrow"),
        P("wide", "narrow", None),
    )
    return jax.shard_map(
        per_device,
        mesh=mesh,
        in_specs=placed,
        out_specs=(P("wide", None, "narrow"), P(None, "wide", None, "narrow")),
        check_vma=False,
    )
```

```python
import jax
import jax.numpy as jnp
from jax import lax
from jax.experimental import pallas as pl
from jax.experimental.pallas import tpu as pltpu
from jax.sharding import PartitionSpec as P

HD = 128


def normalize(values, gain_row):
    values = values.astype(jnp.float32)
    return (
        values
        * lax.rsqrt(jnp.mean(values * values, axis=-1, keepdims=True) + 1e-05)
        * gain_row.astype(jnp.float32)
    )


def rotary(values, positions):
    half_dim = values.shape[-1] // 2
    frequency = 10000.0 ** (-(jnp.arange(half_dim, dtype=jnp.float32) * (2.0 / values.shape[-1])))
    angle = positions[:, None] * frequency[None, :]
    cosine = jnp.cos(angle)[:, None, :]
    sine_part = jnp.sin(angle)[:, None, :]
    first_half = values[..., :half_dim]
    second_half = values[..., half_dim:]
    return jnp.concatenate(
        [
            first_half * cosine - second_half * sine_part,
            second_half * cosine + first_half * sine_part,
        ],
        axis=-1,
    )


TAIL = 128
VMEM_LIMIT = 56 * 1024 * 1024


def places():
    w = lax.axis_index("wide")
    z = lax.axis_index("narrow")
    c = lax.rem(w, 2)
    dx = 2 - 4 * lax.rem(lax.div(w, 2), 2)
    dy = 4 - 8 * lax.div(w, 4)
    first = dx * (1 - c) + dy * c
    second = dy * (1 - c) + dx * c
    return w, z, 1 - 2 * c, first, second


def greet(w, z, sib, first, second):
    barrier = pltpu.get_barrier_semaphore()
    for step in (sib, first, second):
        pl.semaphore_signal(
            barrier, inc=1, device_id={"wide": w + step}, device_id_type=pl.DeviceIdType.MESH
        )
    for k in (1, 2, 3):
        pl.semaphore_signal(
            barrier,
            inc=1,
            device_id={"narrow": lax.rem(z + k, 4)},
            device_id_type=pl.DeviceIdType.MESH,
        )
    pl.semaphore_wait(barrier, 6)


def gather_kernel(rows_ref, gu_ref, out_ref, held, send, recv):
    w, z, sib, first, second = places()
    width = gu_ref.shape[1]
    inner = gu_ref.shape[2] // 2
    experts_held = gu_ref.shape[0]
    experts = experts_held * 8
    mine = (0, first, second, first + second)
    theirs = (sib, sib + second, sib + first, sib + first + second)
    slots = [w + step for step in mine + theirs]
    held[z, w] = rows_ref[...]
    greet(w, z, sib, first, second)
    started = []

    def piece(slot, k, role, device):
        ref = held.at[lax.rem(z + 4 - k, 4), slot]
        return pltpu.make_async_remote_copy(
            src_ref=ref,
            dst_ref=ref,
            send_sem=send.at[len(started)],
            recv_sem=recv.at[role, k],
            device_id=device,
            device_id_type=pl.DeviceIdType.MESH,
        )

    def push(slot, k, role, step):
        copy = piece(slot, k, role, {"wide": w + step})
        copy.start()
        started.append(copy)

    def arrive(role, k):
        ref = held.at[lax.rem(z + 4 - k, 4), slots[role]]
        pltpu.make_async_remote_copy(
            src_ref=ref,
            dst_ref=ref,
            send_sem=send.at[0],
            recv_sem=recv.at[role, k],
            device_id={"wide": w + sib},
            device_id_type=pl.DeviceIdType.MESH,
        ).wait_recv()

    def expert_rows(k):
        group = lax.rem(z + 4 - k, 4)

        def half(h, carry):
            rows = held.shape[2]
            values = held[group, pl.ds(h * 4, 4)]
            inputs = values[:, :, :width].reshape(4 * rows, width)
            tail = values[:, :, width:].reshape(4 * rows, TAIL).astype(jnp.float32)
            lane = lax.broadcasted_iota(jnp.int32, tail.shape, 1)
            for j in range(experts_held):
                e = w * experts_held + j
                hit = (lane == e) | (lane == e + experts) | (lane == e + 2 * experts)
                scale = jnp.sum(jnp.where(hit, tail, 0.0), axis=1, keepdims=True)
                both = jnp.dot(inputs, gu_ref[j], preferred_element_type=jnp.float32)
                gate = both[:, :inner]
                active = gate / (1.0 + jnp.exp(-gate)) * both[:, inner:] * scale
                out_ref[group, pl.ds(h * 4, 4), :, j * inner : (j + 1) * inner] = active.astype(
                    jnp.bfloat16
                ).reshape(4, rows, inner)
            return carry

        lax.fori_loop(0, 2, half, 0)

    for k in (1, 3, 2):
        ref = held.at[z, w]
        copy = pltpu.make_async_remote_copy(
            src_ref=ref,
            dst_ref=ref,
            send_sem=send.at[len(started)],
            recv_sem=recv.at[0, k],
            device_id={"narrow": lax.rem(z + k, 4)},
            device_id_type=pl.DeviceIdType.MESH,
        )
        copy.start()
        started.append(copy)
    order = (0, 1, 3, 2)
    for t in range(7):
        if t < 4:
            k = order[t]
            if k:
                arrive(0, k)
            push(w, k, 1, first)
            push(w, k, 2, second)
            push(w, k, 4, sib)
        if 1 <= t < 5:
            k = order[t - 1]
            arrive(1, k)
            push(slots[1], k, 3, second)
            push(slots[1], k, 5, sib)
            arrive(2, k)
            push(slots[2], k, 6, sib)
        if 2 <= t < 6:
            k = order[t - 2]
            arrive(3, k)
            push(slots[3], k, 7, sib)
        if 3 <= t:
            k = order[t - 3]
            for role in (4, 5, 6, 7):
                arrive(role, k)
            expert_rows(k)
    for copy in started:
        copy.wait_send()


def gather_experts(rows_in, gu):
    rows, padded = rows_in.shape
    held, _, both = gu.shape
    return pl.pallas_call(
        gather_kernel,
        out_shape=jax.ShapeDtypeStruct((4, 8, rows, held * both // 2), jnp.bfloat16),
        in_specs=[pl.BlockSpec(memory_space=pltpu.VMEM)] * 2,
        out_specs=pl.BlockSpec(memory_space=pltpu.VMEM),
        scratch_shapes=[
            pltpu.VMEM((4, 8, rows, padded), jnp.bfloat16),
            pltpu.SemaphoreType.DMA((31,)),
            pltpu.SemaphoreType.DMA((8, 4)),
        ],
        compiler_params=pltpu.CompilerParams(
            collective_id=0, has_side_effects=True, vmem_limit_bytes=VMEM_LIMIT
        ),
        name="gather_experts",
    )(rows_in, gu)


def reduce_kernel(
    weighted_ref,
    down_ref,
    after_ref,
    out_ref,
    sib_out,
    sib_in,
    first_out,
    first_keep,
    first_in,
    second_out,
    second_keep,
    second_in,
    z_out,
    z_in,
    after_in,
    total,
    send,
    recv,
):
    w, z, sib, first, second = places()
    span, cols = out_ref.shape
    rows = after_ref.shape[0]
    mine = (0, first, second, first + second)
    theirs = (sib, sib + second, sib + first, sib + first + second)
    greet(w, z, sib, first, second)
    started = []

    def push(src, dst, number, device):
        copy = pltpu.make_async_remote_copy(
            src_ref=src,
            dst_ref=dst,
            send_sem=send.at[number],
            recv_sem=recv.at[number],
            device_id=device,
            device_id_type=pl.DeviceIdType.MESH,
        )
        copy.start()
        started.append(copy)

    def arrive(dst, number):
        pltpu.make_async_remote_copy(
            src_ref=dst,
            dst_ref=dst,
            send_sem=send.at[number],
            recv_sem=recv.at[number],
            device_id={"wide": w + sib},
            device_id_type=pl.DeviceIdType.MESH,
        ).wait_recv()

    def columns(k):
        return pl.ds(pl.multiple_of(lax.rem(z + k, 4) * cols, cols), cols)

    def product(slot, k):
        values = weighted_ref[:, slot].reshape(span, weighted_ref.shape[3])
        return jnp.dot(values, down_ref[:, columns(k)], preferred_element_type=jnp.float32)

    for k in (1, 3, 2):
        push(
            after_ref.at[:, columns(k)],
            after_in.at[k],
            20 + k,
            {"narrow": lax.rem(z + k, 4)},
        )
    order = (2, 1, 3, 0)
    for t in range(7):
        if t < 4:
            k = order[t]
            for r in range(4):
                sib_out[k, r] = product(w + theirs[r], k).astype(jnp.bfloat16)
            push(sib_out.at[k], sib_in.at[k], k, {"wide": w + sib})
        if 1 <= t < 5:
            k = order[t - 1]
            arrive(sib_in.at[k], k)
            for spot, r in ((0, 1), (1, 3)):
                value = product(w + mine[r], k) + sib_in[k, r].astype(jnp.float32)
                first_out[k, spot] = value.astype(jnp.bfloat16)
            push(first_out.at[k], first_in.at[k], 4 + k, {"wide": w + first})
            for spot, r in ((0, 0), (1, 2)):
                first_keep[k, spot] = product(w + mine[r], k) + sib_in[k, r].astype(jnp.float32)
        if 2 <= t < 6:
            k = order[t - 2]
            arrive(first_in.at[k], 4 + k)
            second_out[k] = (first_keep[k, 1] + first_in[k, 1].astype(jnp.float32)).astype(
                jnp.bfloat16
            )
            push(second_out.at[k], second_in.at[k], 8 + k, {"wide": w + second})
            second_keep[k] = first_keep[k, 0] + first_in[k, 0].astype(jnp.float32)
        if 3 <= t:
            k = order[t - 3]
            arrive(second_in.at[k], 8 + k)
            value = second_keep[k] + second_in[k].astype(jnp.float32)
            if k:
                z_out[k] = value.astype(jnp.bfloat16)
                push(z_out.at[k], z_in.at[k], 12 + k, {"narrow": lax.rem(z + k, 4)})
            else:
                total[...] = value
    for k in (1, 2, 3):
        arrive(z_in.at[k], 12 + k)
        arrive(after_in.at[k], 20 + k)
    total[...] = total[...] + (
        z_in[1].astype(jnp.float32) + z_in[2].astype(jnp.float32) + z_in[3].astype(jnp.float32)
    )
    for k in range(4):
        block = pl.ds(pl.multiple_of(lax.rem(z + 4 - k, 4) * rows, rows), rows)
        own = after_in[k] if k else after_ref[:, columns(0)]
        out_ref[block, :] = (total[block, :] + own.astype(jnp.float32)).astype(jnp.bfloat16)
    for copy in started:
        copy.wait_send()


def reduce_experts(weighted, down, after_rows):
    rows, width = after_rows.shape
    span, cols = rows * 4, width // 4
    half = jnp.bfloat16
    return pl.pallas_call(
        reduce_kernel,
        out_shape=jax.ShapeDtypeStruct((span, cols), half),
        in_specs=[pl.BlockSpec(memory_space=pltpu.VMEM)] * 3,
        out_specs=pl.BlockSpec(memory_space=pltpu.VMEM),
        scratch_shapes=[
            pltpu.VMEM((4, 4, span, cols), half),
            pltpu.VMEM((4, 4, span, cols), half),
            pltpu.VMEM((4, 2, span, cols), half),
            pltpu.VMEM((4, 2, span, cols), jnp.float32),
            pltpu.VMEM((4, 2, span, cols), half),
            pltpu.VMEM((4, span, cols), half),
            pltpu.VMEM((4, span, cols), jnp.float32),
            pltpu.VMEM((4, span, cols), half),
            pltpu.VMEM((4, span, cols), half),
            pltpu.VMEM((4, span, cols), half),
            pltpu.VMEM((4, rows, cols), half),
            pltpu.VMEM((span, cols), jnp.float32),
            pltpu.SemaphoreType.DMA((24,)),
            pltpu.SemaphoreType.DMA((24,)),
        ],
        compiler_params=pltpu.CompilerParams(
            collective_id=1, has_side_effects=True, vmem_limit_bytes=VMEM_LIMIT
        ),
        name="reduce_experts",
    )(weighted, down, after_rows)


def router_table(routes, gate_w, experts):
    named = routes[:, :, None] == jnp.arange(experts, dtype=jnp.int32)[None, None, :]
    return jnp.sum(jnp.where(named, gate_w[:, :, None], 0.0), axis=1)


def in_three(values):
    high = values.astype(jnp.bfloat16)
    rest = values - high.astype(jnp.float32)
    middle = rest.astype(jnp.bfloat16)
    low = (rest - middle.astype(jnp.float32)).astype(jnp.bfloat16)
    return [high, middle, low]


def attend_kernel(
    length_ref,
    hidden_ref,
    gain_ref,
    qk_gain_ref,
    cosine_ref,
    sine_ref,
    tail_ref,
    w_qkv_any,
    cache_any,
    w_out_any,
    rows_ref,
    after_ref,
    fresh_ref,
    pieces,
    w_qkv,
    cache,
    w_out,
    projected,
    squares,
    heads,
    product,
    right_out,
    right_in,
    left_out,
    left_in,
    loads,
    send,
    recv,
    stat_send_ref,
    stat_sems,
    stat_in_ref,
    stat_in_sems,
    sum_send,
    sum_recv,
):
    z = lax.axis_index("narrow")
    span, cols = hidden_ref.shape
    rows, width = after_ref.shape
    copies = [
        pltpu.make_async_copy(w_qkv_any, w_qkv, loads.at[0]),
        pltpu.make_async_copy(cache_any, cache, loads.at[1]),
        pltpu.make_async_copy(w_out_any, w_out, loads.at[2]),
    ]
    for copy in copies:
        copy.start()
    barrier = pltpu.get_barrier_semaphore()
    for k in (1, 2, 3):
        pl.semaphore_signal(
            barrier,
            inc=1,
            device_id={"narrow": lax.rem(z + k, 4)},
            device_id_type=pl.DeviceIdType.MESH,
        )
    pieces[z] = hidden_ref[...]
    pl.semaphore_wait(barrier, 3)

    def remote(src, dst, send_sem, recv_sem, target):
        return pltpu.make_async_remote_copy(
            src_ref=src,
            dst_ref=dst,
            send_sem=send_sem,
            recv_sem=recv_sem,
            device_id={"narrow": target},
            device_id_type=pl.DeviceIdType.MESH,
        )

    def hop(way, s):
        d = (way + 1) // 2
        spot = pieces.at[lax.rem(z - way * s + 4, 4)]
        return remote(spot, spot, send.at[d, s], recv.at[d, s], lax.rem(z + way + 4, 4))

    def can_send(way, s):
        return (z + way >= 0) & (z + way <= 3) & (z - way * s >= 0) & (z - way * s <= 3)

    def has_come(way, s):
        return (z - way * (s + 1) >= 0) & (z - way * (s + 1) <= 3)

    def arrival(way, s):
        d = (way + 1) // 2
        spot = pieces.at[lax.rem(z - way * (s + 1) + 4, 4)]
        return remote(spot, spot, send.at[d, s], recv.at[d, s], lax.rem(z + 1, 4))

    def begin(way, s):
        @pl.when(can_send(way, s))
        def _():
            hop(way, s).start()

    begin(1, 0)
    begin(-1, 0)

    def contribute(src, start):
        values = pieces[src].astype(jnp.float32)
        at = pl.ds(pl.multiple_of(src * cols, cols), cols)
        scaled = (values * gain_ref[0:1, at].astype(jnp.float32)).astype(jnp.bfloat16)
        square = jnp.sum(values * values, axis=1, keepdims=True)
        for i in range(3):
            term = jnp.dot(scaled, w_qkv[i, at, :], preferred_element_type=jnp.float32)
            projected[i] = term if start else projected[i] + term
        wide = jnp.broadcast_to(square, squares.shape)
        squares[...] = wide if start else squares[...] + wide

    copies[0].wait()
    contribute(z, True)
    for s in range(3):
        for way in (1, -1):

            @pl.when(has_come(way, s))
            def _(way=way, s=s):
                arrival(way, s).wait_recv()

            if s < 2:
                begin(way, s + 1)

    def rest(k, carry):
        contribute(lax.rem(z + k, 4), False)
        return carry

    lax.fori_loop(1, 4, rest, 0)
    scale = lax.rsqrt(squares[:, :1] / width + 1e-05)
    for i in range(3):
        projected[i] = projected[i] * scale
    lane = lax.broadcasted_iota(jnp.int32, (span, 128), 1)
    both = [jnp.sum(projected[i] * projected[i], axis=1, keepdims=True) for i in range(2)]
    table = jnp.where(lane == 0, both[0], jnp.where(lane == 1, both[1], 0.0))
    stat_send_ref[...] = table.T[:8]
    outgoing = [
        remote(
            stat_send_ref,
            stat_in_ref.at[k],
            stat_sems.at[k],
            stat_in_sems.at[k],
            lax.rem(z + k, 4),
        )
        for k in (1, 2, 3)
    ]
    for copy in outgoing:
        copy.start()
    fresh_ref[1] = projected[2].astype(jnp.bfloat16)
    for copy in outgoing:
        copy.wait_recv()
    totals = stat_send_ref[...] + stat_in_ref[1] + stat_in_ref[2] + stat_in_ref[3]
    column = jnp.concatenate([totals, jnp.zeros((120, span), jnp.float32)], 0).T
    scales = lax.rsqrt(column / width + 1e-05)
    for copy in outgoing:
        copy.wait_send()
    projected[0] = projected[0] * scales[:, 0:1] * qk_gain_ref[0:1, :]
    projected[1] = projected[1] * scales[:, 1:2] * qk_gain_ref[1:2, :]
    copies[1].wait()
    length = length_ref[0]
    stored = cache.shape[1]
    old_allowed = lax.broadcasted_iota(jnp.int32, (1, stored), 1) < length
    new_allowed = lax.broadcasted_iota(jnp.int32, (span, span), 1) <= lax.broadcasted_iota(
        jnp.int32, (span, span), 0
    )
    across = (((1,), (1,)), ((), ()))

    def head(h, carry):
        at = pl.ds(pl.multiple_of(h * HD, HD), HD)
        cosine, sine = cosine_ref[...], sine_ref[...]

        def turned(i):
            values = projected[i, :, at]
            return (values * cosine + pltpu.roll(values, HD // 2, 1) * sine).astype(jnp.bfloat16)

        query, key = turned(0), turned(1)
        fresh_ref[0, :, at] = key
        old = lax.dot_general(query, cache[0, :, at], across, preferred_element_type=jnp.float32)
        new = lax.dot_general(query, key, across, preferred_element_type=jnp.float32)
        old = jnp.where(old_allowed, old * HD ** (-0.5), -1e30)
        new = jnp.where(new_allowed, new * HD ** (-0.5), -1e30)
        highest = jnp.maximum(
            jnp.max(old, axis=1, keepdims=True), jnp.max(new, axis=1, keepdims=True)
        )
        old, new = jnp.exp(old - highest), jnp.exp(new - highest)
        denominator = jnp.sum(old, axis=1, keepdims=True) + jnp.sum(new, axis=1, keepdims=True)
        summed = jnp.dot(
            old.astype(jnp.bfloat16), cache[1, :, at], preferred_element_type=jnp.float32
        ) + jnp.dot(
            new.astype(jnp.bfloat16), fresh_ref[1, :, at], preferred_element_type=jnp.float32
        )
        heads[:, at] = (summed / denominator).astype(jnp.bfloat16)
        return carry

    lax.fori_loop(0, cols // HD, head, 0)
    copies[2].wait()

    def project(i, carry):
        at = pl.ds(pl.multiple_of(i * cols, cols), cols)
        product[:, :, at] = jnp.dot(
            heads[...], w_out[:, at], preferred_element_type=jnp.float32
        ).reshape(4, rows, cols)
        return carry

    lax.fori_loop(0, width // cols, project, 0)

    def onward(way, d):
        out, into = (right_out, right_in) if way > 0 else (left_out, left_in)
        side = (way + 1) // 2
        return remote(
            out.at[d], into.at[d], sum_send.at[side, d], sum_recv.at[side, d], lax.rem(z + way + 4, 4)
        )

    def passing(way, d):
        return z < d if way > 0 else z > d

    for right, left in ((3, 0), (2, 1), (1, 2)):
        for way, d in ((1, right), (-1, left)):
            out, into = (right_out, right_in) if way > 0 else (left_out, left_in)
            first = z == 0 if way > 0 else z == 3

            @pl.when(passing(way, d) & first)
            def _(way=way, d=d, out=out):
                out[d] = product[d].astype(jnp.bfloat16)
                onward(way, d).start()

            @pl.when(passing(way, d) & jnp.logical_not(first))
            def _(way=way, d=d, out=out, into=into):
                onward(way, d).wait_recv()
                out[d] = (product[d] + into[d].astype(jnp.float32)).astype(jnp.bfloat16)
                onward(way, d).start()

    @pl.when(z > 0)
    def _():
        onward(1, z).wait_recv()
        product[z] = product[z] + right_in[z].astype(jnp.float32)

    @pl.when(z < 3)
    def _():
        onward(-1, z).wait_recv()
        product[z] = product[z] + left_in[z].astype(jnp.float32)

    own = pl.ds(pl.multiple_of(z * rows, rows), rows)
    tokens = jnp.concatenate([pieces[i, own, :] for i in range(4)], 1).astype(jnp.float32)
    after = (tokens + product[z].astype(jnp.bfloat16).astype(jnp.float32)).astype(jnp.bfloat16)
    after_ref[...] = after
    after = after.astype(jnp.float32)
    mean = jnp.mean(after * after, axis=1, keepdims=True)
    rows_ref[:, :width] = (
        after * lax.rsqrt(mean + 1e-05) * gain_ref[1:2, :].astype(jnp.float32)
    ).astype(jnp.bfloat16)
    rows_ref[:, width:] = tail_ref[...]
    for way in (1, -1):
        for s in range(3):

            @pl.when(can_send(way, s))
            def _(way=way, s=s):
                hop(way, s).wait_send()

        for d in (1, 2, 3) if way > 0 else (0, 1, 2):

            @pl.when(passing(way, d))
            def _(way=way, d=d):
                onward(way, d).wait_send()


def attend(length, hidden, norm_gain, qk_gain, cosine, sine, tail, w_qkv, cache, w_out):
    span, cols = hidden.shape
    width = cols * 4
    rows = span // 4
    half = jnp.bfloat16
    vmem = pl.BlockSpec(memory_space=pltpu.VMEM)
    anywhere = pl.BlockSpec(memory_space=pl.ANY)
    dma = pltpu.SemaphoreType.DMA
    return pl.pallas_call(
        attend_kernel,
        out_shape=(
            jax.ShapeDtypeStruct((rows, width + TAIL), half),
            jax.ShapeDtypeStruct((rows, width), half),
            jax.ShapeDtypeStruct((2, span, cols), half),
        ),
        in_specs=[pl.BlockSpec(memory_space=pltpu.SMEM)] + [vmem] * 6 + [anywhere] * 3,
        out_specs=(vmem, vmem, vmem),
        scratch_shapes=[
            pltpu.VMEM((4, span, cols), half),
            pltpu.VMEM(w_qkv.shape, half),
            pltpu.VMEM(cache.shape, half),
            pltpu.VMEM(w_out.shape, half),
            pltpu.VMEM((3, span, cols), jnp.float32),
            pltpu.VMEM((span, 128), jnp.float32),
            pltpu.VMEM((span, cols), half),
            pltpu.VMEM((4, rows, width), jnp.float32),
            pltpu.VMEM((4, rows, width), half),
            pltpu.VMEM((4, rows, width), half),
            pltpu.VMEM((4, rows, width), half),
            pltpu.VMEM((4, rows, width), half),
            dma((3,)),
            dma((2, 3)),
            dma((2, 3)),
            pltpu.VMEM((8, span), jnp.float32),
            dma((4,)),
            pltpu.VMEM((4, 8, span), jnp.float32),
            dma((4,)),
            dma((2, 4)),
            dma((2, 4)),
        ],
        compiler_params=pltpu.CompilerParams(
            collective_id=2, has_side_effects=True, vmem_limit_bytes=VMEM_LIMIT
        ),
        name="attend",
    )(length, hidden, norm_gain, qk_gain, cosine, sine, tail, w_qkv, cache, w_out)


def layer_by_copies(
    hidden, norm_gain, w_qkv, qk_gain, w_out, cache, lengths, placing, routes, gate_w, w_gu, w_down
):
    position = lax.axis_index("wide")
    column = lax.axis_index("narrow")
    span = hidden.shape[1]
    rows, width = span // 4, hidden.shape[2] * 4
    held, _, _, inner = w_gu.shape
    length = jnp.sum(
        jnp.where(jnp.arange(lengths.shape[0], dtype=jnp.int32) == placing[position], lengths, 0)
    )
    positions = length.astype(jnp.float32) + jnp.arange(span, dtype=jnp.float32)
    frequency = 10000.0 ** (-(jnp.arange(HD // 2, dtype=jnp.float32) * (2.0 / HD)))
    angle = positions[:, None] * frequency[None, :]
    cosine, sine = jnp.cos(angle), jnp.sin(angle)
    table = router_table(
        lax.dynamic_slice_in_dim(routes[0], column * rows, rows, 0),
        lax.dynamic_slice_in_dim(gate_w[0], column * rows, rows, 0),
        held * 8,
    )
    filler = jnp.zeros((rows, TAIL - 24 * held), jnp.bfloat16)
    rows_in, after_rows, fresh = attend(
        length.reshape(1),
        hidden[0],
        norm_gain,
        qk_gain,
        jnp.concatenate([cosine, cosine], 1),
        jnp.concatenate([-sine, sine], 1),
        jnp.concatenate(in_three(table) + [filler], 1),
        jnp.transpose(w_qkv, (1, 0, 2)),
        cache[:, 0],
        w_out,
    )
    weighted = gather_experts(rows_in, w_gu.reshape(held, width, 2 * inner))
    result = reduce_experts(weighted, w_down.reshape(held * inner, width), after_rows)
    return result[None], fresh[:, None]


def experts_by_collectives(after_rows, gain, routes, gate_w, w_gu, w_down):
    position = lax.axis_index("wide")
    column = lax.axis_index("narrow")
    wide_size = lax.axis_size("wide")
    narrow = lax.axis_size("narrow")
    rows, full_width = after_rows.shape
    span_len, share_cols = rows * narrow, full_width // narrow
    after_all = lax.all_gather(after_rows, ("wide", "narrow"), axis=0, tiled=True)
    after_own = lax.dynamic_slice(
        after_all, (position * span_len, column * share_cols), (span_len, share_cols)
    )
    routed = normalize(after_all, gain).astype(jnp.bfloat16)
    held_experts = w_gu.shape[0]
    inner_cols = w_gu.shape[3]
    experts = held_experts * wide_size
    table = router_table(routes, gate_w, experts)
    table = lax.all_gather(table, "wide", axis=0, tiled=True)
    scale = lax.dynamic_slice_in_dim(table, position * held_experts, held_experts, 1)
    pieces = []
    for j in range(held_experts):
        gate_up = jnp.dot(
            routed,
            w_gu[j].reshape(full_width, 2 * inner_cols),
            preferred_element_type=jnp.float32,
        )
        activated = jax.nn.silu(gate_up[:, :inner_cols]) * gate_up[:, inner_cols:]
        pieces.append((activated * scale[:, j : j + 1]).astype(jnp.bfloat16))
    weighted = jnp.concatenate(pieces, 1)
    combined = jnp.dot(
        weighted,
        w_down.reshape(held_experts * inner_cols, full_width),
        preferred_element_type=jnp.float32,
    ).astype(jnp.bfloat16)
    combined = lax.psum_scatter(combined, "wide", scatter_dimension=0, tiled=True)
    expert_out = lax.psum_scatter(
        combined, "narrow", scatter_dimension=1, tiled=True
    ).astype(jnp.float32)
    return (after_own.astype(jnp.float32) + expert_out).astype(jnp.bfloat16)

def per_device(
    hidden, norm_gain, w_qkv, qk_gain, w_out, cache, lengths, placing, routes, gate_w, w_gu, w_down
):
    narrow = lax.axis_size("narrow")
    column = lax.axis_index("narrow")
    position = lax.axis_index("wide")
    span_len = hidden.shape[1]
    share_cols = hidden.shape[2]
    full_width = share_cols * narrow
    tokens = lax.all_gather(hidden[0], "narrow", axis=1, tiled=True)
    normed = normalize(tokens, norm_gain[0]).astype(jnp.bfloat16)
    local_cols = w_qkv.shape[2]
    projected = jnp.dot(
        normed, w_qkv.reshape(full_width, 3 * local_cols), preferred_element_type=jnp.float32
    )
    queries = projected[:, :local_cols]
    keys_new = projected[:, local_cols : 2 * local_cols]
    values_new = projected[:, 2 * local_cols :]
    squares = lax.psum((jnp.sum(queries * queries, -1), jnp.sum(keys_new * keys_new, -1)), "narrow")
    features = local_cols * narrow
    queries = queries * lax.rsqrt(squares[0][:, None] / features + 1e-05) * qk_gain[0]
    keys_new = keys_new * lax.rsqrt(squares[1][:, None] / features + 1e-05) * qk_gain[1]
    head_count = local_cols // HD
    length = lengths[placing[position]]
    positions = length.astype(jnp.float32) + jnp.arange(span_len, dtype=jnp.float32)
    queries = rotary(queries.reshape(span_len, head_count, HD), positions).astype(jnp.bfloat16)
    keys_new = rotary(keys_new.reshape(span_len, head_count, HD), positions).astype(jnp.bfloat16)
    values_new = values_new.reshape(span_len, head_count, HD).astype(jnp.bfloat16)
    stored = cache.shape[2]
    all_keys = jnp.concatenate([cache[0, 0].reshape(stored, head_count, HD), keys_new], 0)
    all_values = jnp.concatenate([cache[1, 0].reshape(stored, head_count, HD), values_new], 0)
    scores = jnp.einsum(
        "thd,jhd->htj", queries, all_keys, preferred_element_type=jnp.float32
    ) * HD ** (-0.5)
    key_index = jnp.arange(stored + span_len, dtype=jnp.int32)[None, :]
    query_index = jnp.arange(span_len, dtype=jnp.int32)[:, None]
    allowed = jnp.where(key_index < stored, key_index < length, key_index - stored <= query_index)
    scores = jnp.where(allowed[None], scores, -1e30)
    highest = jnp.max(scores, axis=-1, keepdims=True)
    exponent = jnp.exp(scores - highest)
    weights = exponent.astype(jnp.bfloat16)
    denominator = jnp.sum(exponent, axis=-1)
    summed = jnp.einsum("htj,jhd->thd", weights, all_values, preferred_element_type=jnp.float32)
    heads_out = (
        (summed / jnp.transpose(denominator)[:, :, None])
        .astype(jnp.bfloat16)
        .reshape(span_len, local_cols)
    )
    partial_out = jnp.dot(heads_out, w_out, preferred_element_type=jnp.float32)
    rows = span_len // narrow
    attention = lax.psum_scatter(
        partial_out.astype(jnp.bfloat16), "narrow", scatter_dimension=0, tiled=True
    ).astype(jnp.float32)
    own_rows = lax.dynamic_slice_in_dim(tokens, column * rows, rows, 0)
    after_rows = (own_rows.astype(jnp.float32) + attention).astype(jnp.bfloat16)
    result = experts_by_collectives(
        after_rows, norm_gain[1], routes[0], gate_w[0], w_gu, w_down
    )[None]
    fresh = jnp.stack(
        [keys_new.reshape(span_len, local_cols), values_new.reshape(span_len, local_cols)]
    )[:, None]
    return (result, fresh)


def solution(mesh):
    placed = (
        P("wide", None, "narrow"),
        P(),
        P(None, None, "narrow"),
        P(None, "narrow"),
        P("narrow", None),
        P(None, "wide", None, "narrow"),
        P(),
        P(),
        P("wide", None, None),
        P("wide", None, None),
        P("wide", None, None, "narrow"),
        P("wide", "narrow", None),
    )
    by_copies = mesh.shape["wide"] == 8 and mesh.shape["narrow"] == 4
    return jax.shard_map(
        layer_by_copies if by_copies else per_device,
        mesh=mesh,
        in_specs=placed,
        out_specs=(P("wide", None, "narrow"), P(None, "wide", None, "narrow")),
        check_vma=False,
    )
```

```python
import jax
import jax.numpy as jnp
from jax import lax
from jax.experimental import pallas as pl
from jax.experimental.pallas import tpu as pltpu
from jax.sharding import PartitionSpec as P

HD = 128


def normalize(values, gain_row):
    values = values.astype(jnp.float32)
    return (
        values
        * lax.rsqrt(jnp.mean(values * values, axis=-1, keepdims=True) + 1e-05)
        * gain_row.astype(jnp.float32)
    )


def rotary(values, positions):
    half_dim = values.shape[-1] // 2
    frequency = 10000.0 ** (-(jnp.arange(half_dim, dtype=jnp.float32) * (2.0 / values.shape[-1])))
    angle = positions[:, None] * frequency[None, :]
    cosine = jnp.cos(angle)[:, None, :]
    sine_part = jnp.sin(angle)[:, None, :]
    first_half = values[..., :half_dim]
    second_half = values[..., half_dim:]
    return jnp.concatenate(
        [
            first_half * cosine - second_half * sine_part,
            second_half * cosine + first_half * sine_part,
        ],
        axis=-1,
    )


TAIL = 128
PARTS = 2
VMEM_LIMIT = 56 * 1024 * 1024


def places():
    w = lax.axis_index("wide")
    z = lax.axis_index("narrow")
    c = lax.rem(w, 2)
    dx = 2 - 4 * lax.rem(lax.div(w, 2), 2)
    dy = 4 - 8 * lax.div(w, 4)
    first = dx * (1 - c) + dy * c
    second = dy * (1 - c) + dx * c
    return w, z, 1 - 2 * c, first, second


def greet(w, z, sib, first, second):
    barrier = pltpu.get_barrier_semaphore()
    for step in (sib, first, second):
        pl.semaphore_signal(
            barrier, inc=1, device_id={"wide": w + step}, device_id_type=pl.DeviceIdType.MESH
        )
    for k in (1, 2, 3):
        pl.semaphore_signal(
            barrier,
            inc=1,
            device_id={"narrow": lax.rem(z + k, 4)},
            device_id_type=pl.DeviceIdType.MESH,
        )
    pl.semaphore_wait(barrier, 6)


def gather_kernel(rows_ref, gu_ref, out_ref, held, send, recv, z_send, z_recv):
    w, z, sib, first, second = places()
    width = gu_ref.shape[1]
    inner = gu_ref.shape[2] // 2
    experts_held = gu_ref.shape[0]
    experts = experts_held * 8
    mine = (0, first, second, first + second)
    theirs = (sib, sib + second, sib + first, sib + first + second)
    slots = [w + step for step in mine + theirs]
    held[z, w] = rows_ref[...]
    greet(w, z, sib, first, second)
    started = []
    upper = lax.div(z, 2)
    order = (z, z + 1 - 2 * lax.rem(z, 2), 2 - upper, 3 - 3 * upper)

    def piece(slot, k, role, device):
        ref = held.at[order[k], slot]
        return pltpu.make_async_remote_copy(
            src_ref=ref,
            dst_ref=ref,
            send_sem=send.at[len(started)],
            recv_sem=recv.at[role, k],
            device_id=device,
            device_id_type=pl.DeviceIdType.MESH,
        )

    def push(slot, k, role, step):
        copy = piece(slot, k, role, {"wide": w + step})
        copy.start()
        started.append(copy)

    def arrive(role, k):
        ref = held.at[order[k], slots[role]]
        pltpu.make_async_remote_copy(
            src_ref=ref,
            dst_ref=ref,
            send_sem=send.at[0],
            recv_sem=recv.at[role, k],
            device_id={"wide": w + sib},
            device_id_type=pl.DeviceIdType.MESH,
        ).wait_recv()

    def expert_rows(k):
        group = order[k]

        def half(h, carry):
            rows = held.shape[2]
            values = held[group, pl.ds(h * 4, 4)]
            inputs = values[:, :, :width].reshape(4 * rows, width)
            tail = values[:, :, width:].reshape(4 * rows, TAIL).astype(jnp.float32)
            lane = lax.broadcasted_iota(jnp.int32, tail.shape, 1)
            for j in range(experts_held):
                e = w * experts_held + j
                hit = (lane == e) | (lane == e + experts) | (lane == e + 2 * experts)
                scale = jnp.sum(jnp.where(hit, tail, 0.0), axis=1, keepdims=True)
                both = jnp.dot(inputs, gu_ref[j], preferred_element_type=jnp.float32)
                gate = both[:, :inner]
                active = gate / (1.0 + jnp.exp(-gate)) * both[:, inner:] * scale
                out_ref[group, pl.ds(h * 4, 4), :, j * inner : (j + 1) * inner] = active.astype(
                    jnp.bfloat16
                ).reshape(4, rows, inner)
            return carry

        lax.fori_loop(0, 2, half, 0)

    def along(src, way):
        ref = held.at[src, w]
        return pltpu.make_async_remote_copy(
            src_ref=ref,
            dst_ref=ref,
            send_sem=z_send.at[(way + 1) // 2, src],
            recv_sem=z_recv.at[src],
            device_id={"narrow": lax.rem(z + way + 4, 4)},
            device_id_type=pl.DeviceIdType.MESH,
        )

    def sends(src, way):
        return (src <= z) & (z < 3) if way > 0 else (src >= z) & (z > 0)

    def pass_on(src):
        for way in (1, -1):

            @pl.when(sends(src, way))
            def _(way=way):
                along(src, way).start()

    pass_on(z)
    for t in range(7):
        if t < 4:
            push(w, t, 1, first)
            push(w, t, 2, second)
            push(w, t, 4, sib)
        if t < 3:
            along(order[t + 1], 1).wait_recv()
            pass_on(order[t + 1])
        if 1 <= t < 5:
            k = t - 1
            arrive(1, k)
            push(slots[1], k, 3, second)
            push(slots[1], k, 5, sib)
            arrive(2, k)
            push(slots[2], k, 6, sib)
        if 2 <= t < 6:
            k = t - 2
            arrive(3, k)
            push(slots[3], k, 7, sib)
        if 3 <= t:
            for role in (4, 5, 6, 7):
                arrive(role, t - 3)
            expert_rows(t - 3)
    for copy in started:
        copy.wait_send()
    for src in order:
        for way in (1, -1):

            @pl.when(sends(src, way))
            def _(src=src, way=way):
                along(src, way).wait_send()


def gather_experts(rows_in, gu):
    rows, padded = rows_in.shape
    held, _, both = gu.shape
    return pl.pallas_call(
        gather_kernel,
        out_shape=jax.ShapeDtypeStruct((4, 8, rows, held * both // 2), jnp.bfloat16),
        in_specs=[pl.BlockSpec(memory_space=pltpu.VMEM)] * 2,
        out_specs=pl.BlockSpec(memory_space=pltpu.VMEM),
        scratch_shapes=[
            pltpu.VMEM((4, 8, rows, padded), jnp.bfloat16),
            pltpu.SemaphoreType.DMA((28,)),
            pltpu.SemaphoreType.DMA((8, 4)),
            pltpu.SemaphoreType.DMA((2, 4)),
            pltpu.SemaphoreType.DMA((4,)),
        ],
        compiler_params=pltpu.CompilerParams(
            collective_id=0, has_side_effects=True, vmem_limit_bytes=VMEM_LIMIT
        ),
        name="gather_experts",
    )(rows_in, gu)


def reduce_kernel(
    weighted_ref,
    down_ref,
    after_ref,
    out_ref,
    sib_out,
    sib_in,
    first_out,
    first_keep,
    first_in,
    second_out,
    second_keep,
    second_in,
    z_out,
    z_in,
    after_in,
    total,
    send,
    recv,
):
    w, z, sib, first, second = places()
    span, cols = out_ref.shape
    rows = after_ref.shape[0]
    mine = (0, first, second, first + second)
    theirs = (sib, sib + second, sib + first, sib + first + second)
    greet(w, z, sib, first, second)
    started = []

    def push(src, dst, number, device):
        copy = pltpu.make_async_remote_copy(
            src_ref=src,
            dst_ref=dst,
            send_sem=send.at[number],
            recv_sem=recv.at[number],
            device_id=device,
            device_id_type=pl.DeviceIdType.MESH,
        )
        copy.start()
        started.append(copy)

    def arrive(dst, number):
        pltpu.make_async_remote_copy(
            src_ref=dst,
            dst_ref=dst,
            send_sem=send.at[number],
            recv_sem=recv.at[number],
            device_id={"wide": w + sib},
            device_id_type=pl.DeviceIdType.MESH,
        ).wait_recv()

    share = cols // PARTS

    def columns(k):
        return pl.ds(pl.multiple_of(lax.rem(z + k, 4) * cols, cols), cols)

    def product(slot, k):
        start = lax.rem(z + k // PARTS, 4) * cols + k % PARTS * share
        values = weighted_ref[:, slot].reshape(span, weighted_ref.shape[3])
        return jnp.dot(
            values,
            down_ref[:, pl.ds(pl.multiple_of(start, share), share)],
            preferred_element_type=jnp.float32,
        )

    for k in (1, 3, 2):
        push(
            after_ref.at[:, columns(k)],
            after_in.at[k],
            16 * PARTS + k,
            {"narrow": lax.rem(z + k, 4)},
        )
    order = [k * PARTS + p for k in (2, 1, 3, 0) for p in range(PARTS)]
    count = len(order)
    for t in range(count + 3):
        if t < count:
            k = order[t]
            for r in range(4):
                sib_out[k, r] = product(w + theirs[r], k).astype(jnp.bfloat16)
            push(sib_out.at[k], sib_in.at[k], k, {"wide": w + sib})
        if 1 <= t < count + 1:
            k = order[t - 1]
            arrive(sib_in.at[k], k)
            for spot, r in ((0, 1), (1, 3)):
                value = product(w + mine[r], k) + sib_in[k, r].astype(jnp.float32)
                first_out[k, spot] = value.astype(jnp.bfloat16)
            push(first_out.at[k], first_in.at[k], 4 * PARTS + k, {"wide": w + first})
            for spot, r in ((0, 0), (1, 2)):
                first_keep[k, spot] = product(w + mine[r], k) + sib_in[k, r].astype(jnp.float32)
        if 2 <= t < count + 2:
            k = order[t - 2]
            arrive(first_in.at[k], 4 * PARTS + k)
            second_out[k] = (first_keep[k, 1] + first_in[k, 1].astype(jnp.float32)).astype(
                jnp.bfloat16
            )
            push(second_out.at[k], second_in.at[k], 8 * PARTS + k, {"wide": w + second})
            second_keep[k] = first_keep[k, 0] + first_in[k, 0].astype(jnp.float32)
        if 3 <= t:
            k = order[t - 3]
            arrive(second_in.at[k], 8 * PARTS + k)
            value = second_keep[k] + second_in[k].astype(jnp.float32)
            if k >= PARTS:
                z_out[k] = value.astype(jnp.bfloat16)
                push(z_out.at[k], z_in.at[k], 12 * PARTS + k, {"narrow": lax.rem(z + k // PARTS, 4)})
            else:
                total[:, k * share : (k + 1) * share] = value
    for k in (1, 2, 3):
        arrive(after_in.at[k], 16 * PARTS + k)
    for n in order[: 3 * PARTS]:
        arrive(z_in.at[n], 12 * PARTS + n)
        at = slice(n % PARTS * share, (n % PARTS + 1) * share)
        total[:, at] = total[:, at] + z_in[n].astype(jnp.float32)
    for k in range(4):
        block = pl.ds(pl.multiple_of(lax.rem(z + 4 - k, 4) * rows, rows), rows)
        own = after_in[k] if k else after_ref[:, columns(0)]
        out_ref[block, :] = (total[block, :] + own.astype(jnp.float32)).astype(jnp.bfloat16)
    for copy in started:
        copy.wait_send()


def reduce_experts(weighted, down, after_rows):
    rows, width = after_rows.shape
    span, cols = rows * 4, width // 4
    parts, share = 4 * PARTS, cols // PARTS
    half = jnp.bfloat16
    return pl.pallas_call(
        reduce_kernel,
        out_shape=jax.ShapeDtypeStruct((span, cols), half),
        in_specs=[pl.BlockSpec(memory_space=pltpu.VMEM)] * 3,
        out_specs=pl.BlockSpec(memory_space=pltpu.VMEM),
        scratch_shapes=[
            pltpu.VMEM((parts, 4, span, share), half),
            pltpu.VMEM((parts, 4, span, share), half),
            pltpu.VMEM((parts, 2, span, share), half),
            pltpu.VMEM((parts, 2, span, share), jnp.float32),
            pltpu.VMEM((parts, 2, span, share), half),
            pltpu.VMEM((parts, span, share), half),
            pltpu.VMEM((parts, span, share), jnp.float32),
            pltpu.VMEM((parts, span, share), half),
            pltpu.VMEM((parts, span, share), half),
            pltpu.VMEM((parts, span, share), half),
            pltpu.VMEM((4, rows, cols), half),
            pltpu.VMEM((span, cols), jnp.float32),
            pltpu.SemaphoreType.DMA((16 * PARTS + 4,)),
            pltpu.SemaphoreType.DMA((16 * PARTS + 4,)),
        ],
        compiler_params=pltpu.CompilerParams(
            collective_id=1, has_side_effects=True, vmem_limit_bytes=VMEM_LIMIT
        ),
        name="reduce_experts",
    )(weighted, down, after_rows)


def router_table(routes, gate_w, experts):
    named = routes[:, :, None] == jnp.arange(experts, dtype=jnp.int32)[None, None, :]
    return jnp.sum(jnp.where(named, gate_w[:, :, None], 0.0), axis=1)


def in_three(values):
    high = values.astype(jnp.bfloat16)
    rest = values - high.astype(jnp.float32)
    middle = rest.astype(jnp.bfloat16)
    low = (rest - middle.astype(jnp.float32)).astype(jnp.bfloat16)
    return [high, middle, low]


def attend_kernel(
    length_ref,
    hidden_ref,
    gain_ref,
    qk_gain_ref,
    cosine_ref,
    sine_ref,
    tail_ref,
    w_qkv_any,
    cache_any,
    w_out_any,
    rows_ref,
    after_ref,
    fresh_ref,
    pieces,
    w_qkv,
    cache,
    w_out,
    projected,
    squares,
    heads,
    product,
    right_out,
    right_in,
    left_out,
    left_in,
    loads,
    send,
    recv,
    stat_send_ref,
    stat_sems,
    stat_in_ref,
    stat_in_sems,
    sum_send,
    sum_recv,
):
    z = lax.axis_index("narrow")
    span, cols = hidden_ref.shape
    rows, width = after_ref.shape
    copies = [
        pltpu.make_async_copy(w_qkv_any, w_qkv, loads.at[0]),
        pltpu.make_async_copy(cache_any, cache, loads.at[1]),
        pltpu.make_async_copy(w_out_any, w_out, loads.at[2]),
    ]
    for copy in copies:
        copy.start()
    barrier = pltpu.get_barrier_semaphore()
    for k in (1, 2, 3):
        pl.semaphore_signal(
            barrier,
            inc=1,
            device_id={"narrow": lax.rem(z + k, 4)},
            device_id_type=pl.DeviceIdType.MESH,
        )
    pieces[z] = hidden_ref[...]
    pl.semaphore_wait(barrier, 3)

    def remote(src, dst, send_sem, recv_sem, target):
        return pltpu.make_async_remote_copy(
            src_ref=src,
            dst_ref=dst,
            send_sem=send_sem,
            recv_sem=recv_sem,
            device_id={"narrow": target},
            device_id_type=pl.DeviceIdType.MESH,
        )

    def hop(way, s):
        d = (way + 1) // 2
        spot = pieces.at[lax.rem(z - way * s + 4, 4)]
        return remote(spot, spot, send.at[d, s], recv.at[d, s], lax.rem(z + way + 4, 4))

    def can_send(way, s):
        return (z + way >= 0) & (z + way <= 3) & (z - way * s >= 0) & (z - way * s <= 3)

    def has_come(way, s):
        return (z - way * (s + 1) >= 0) & (z - way * (s + 1) <= 3)

    def arrival(way, s):
        d = (way + 1) // 2
        spot = pieces.at[lax.rem(z - way * (s + 1) + 4, 4)]
        return remote(spot, spot, send.at[d, s], recv.at[d, s], lax.rem(z + 1, 4))

    def begin(way, s):
        @pl.when(can_send(way, s))
        def _():
            hop(way, s).start()

    begin(1, 0)
    begin(-1, 0)

    def contribute(src, start):
        values = pieces[src].astype(jnp.float32)
        at = pl.ds(pl.multiple_of(src * cols, cols), cols)
        scaled = (values * gain_ref[0:1, at].astype(jnp.float32)).astype(jnp.bfloat16)
        square = jnp.sum(values * values, axis=1, keepdims=True)
        for i in range(3):
            term = jnp.dot(scaled, w_qkv[i, at, :], preferred_element_type=jnp.float32)
            projected[i] = term if start else projected[i] + term
        wide = jnp.broadcast_to(square, squares.shape)
        squares[...] = wide if start else squares[...] + wide

    copies[0].wait()
    contribute(z, True)
    for s in range(3):
        for way in (1, -1):

            @pl.when(has_come(way, s))
            def _(way=way, s=s):
                arrival(way, s).wait_recv()

            if s < 2:
                begin(way, s + 1)

    def rest(k, carry):
        contribute(lax.rem(z + k, 4), False)
        return carry

    lax.fori_loop(1, 4, rest, 0)
    scale = lax.rsqrt(squares[:, :1] / width + 1e-05)
    for i in range(3):
        projected[i] = projected[i] * scale
    lane = lax.broadcasted_iota(jnp.int32, (span, 128), 1)
    both = [jnp.sum(projected[i] * projected[i], axis=1, keepdims=True) for i in range(2)]
    table = jnp.where(lane == 0, both[0], jnp.where(lane == 1, both[1], 0.0))
    stat_send_ref[...] = table.T[:8]
    outgoing = [
        remote(
            stat_send_ref,
            stat_in_ref.at[k],
            stat_sems.at[k],
            stat_in_sems.at[k],
            lax.rem(z + k, 4),
        )
        for k in (1, 2, 3)
    ]
    for copy in outgoing:
        copy.start()
    fresh_ref[1] = projected[2].astype(jnp.bfloat16)
    for copy in outgoing:
        copy.wait_recv()
    totals = stat_send_ref[...] + stat_in_ref[1] + stat_in_ref[2] + stat_in_ref[3]
    column = jnp.concatenate([totals, jnp.zeros((120, span), jnp.float32)], 0).T
    scales = lax.rsqrt(column / width + 1e-05)
    for copy in outgoing:
        copy.wait_send()
    projected[0] = projected[0] * scales[:, 0:1] * qk_gain_ref[0:1, :]
    projected[1] = projected[1] * scales[:, 1:2] * qk_gain_ref[1:2, :]
    copies[1].wait()
    length = length_ref[0]
    stored = cache.shape[1]
    old_allowed = lax.broadcasted_iota(jnp.int32, (1, stored), 1) < length
    new_allowed = lax.broadcasted_iota(jnp.int32, (span, span), 1) <= lax.broadcasted_iota(
        jnp.int32, (span, span), 0
    )
    across = (((1,), (1,)), ((), ()))

    def head(h, carry):
        at = pl.ds(pl.multiple_of(h * HD, HD), HD)
        cosine, sine = cosine_ref[...], sine_ref[...]

        def turned(i):
            values = projected[i, :, at]
            return (values * cosine + pltpu.roll(values, HD // 2, 1) * sine).astype(jnp.bfloat16)

        query, key = turned(0), turned(1)
        fresh_ref[0, :, at] = key
        old = lax.dot_general(query, cache[0, :, at], across, preferred_element_type=jnp.float32)
        new = lax.dot_general(query, key, across, preferred_element_type=jnp.float32)
        old = jnp.where(old_allowed, old * HD ** (-0.5), -1e30)
        new = jnp.where(new_allowed, new * HD ** (-0.5), -1e30)
        highest = jnp.maximum(
            jnp.max(old, axis=1, keepdims=True), jnp.max(new, axis=1, keepdims=True)
        )
        old, new = jnp.exp(old - highest), jnp.exp(new - highest)
        denominator = jnp.sum(old, axis=1, keepdims=True) + jnp.sum(new, axis=1, keepdims=True)
        summed = jnp.dot(
            old.astype(jnp.bfloat16), cache[1, :, at], preferred_element_type=jnp.float32
        ) + jnp.dot(
            new.astype(jnp.bfloat16), fresh_ref[1, :, at], preferred_element_type=jnp.float32
        )
        heads[:, at] = (summed / denominator).astype(jnp.bfloat16)
        return carry

    lax.fori_loop(0, cols // HD, head, 0)
    copies[2].wait()

    def project(i, carry):
        at = pl.ds(pl.multiple_of(i * cols, cols), cols)
        product[:, :, at] = jnp.dot(
            heads[...], w_out[:, at], preferred_element_type=jnp.float32
        ).reshape(4, rows, cols)
        return carry

    lax.fori_loop(0, width // cols, project, 0)

    def onward(way, d):
        out, into = (right_out, right_in) if way > 0 else (left_out, left_in)
        side = (way + 1) // 2
        return remote(
            out.at[d], into.at[d], sum_send.at[side, d], sum_recv.at[side, d], lax.rem(z + way + 4, 4)
        )

    def passing(way, d):
        return z < d if way > 0 else z > d

    for right, left in ((3, 0), (2, 1), (1, 2)):
        for way, d in ((1, right), (-1, left)):
            out, into = (right_out, right_in) if way > 0 else (left_out, left_in)
            first = z == 0 if way > 0 else z == 3

            @pl.when(passing(way, d) & first)
            def _(way=way, d=d, out=out):
                out[d] = product[d].astype(jnp.bfloat16)
                onward(way, d).start()

            @pl.when(passing(way, d) & jnp.logical_not(first))
            def _(way=way, d=d, out=out, into=into):
                onward(way, d).wait_recv()
                out[d] = (product[d] + into[d].astype(jnp.float32)).astype(jnp.bfloat16)
                onward(way, d).start()

    @pl.when(z > 0)
    def _():
        onward(1, z).wait_recv()
        product[z] = product[z] + right_in[z].astype(jnp.float32)

    @pl.when(z < 3)
    def _():
        onward(-1, z).wait_recv()
        product[z] = product[z] + left_in[z].astype(jnp.float32)

    own = pl.ds(pl.multiple_of(z * rows, rows), rows)
    tokens = jnp.concatenate([pieces[i, own, :] for i in range(4)], 1).astype(jnp.float32)
    after = (tokens + product[z].astype(jnp.bfloat16).astype(jnp.float32)).astype(jnp.bfloat16)
    after_ref[...] = after
    after = after.astype(jnp.float32)
    mean = jnp.mean(after * after, axis=1, keepdims=True)
    rows_ref[:, :width] = (
        after * lax.rsqrt(mean + 1e-05) * gain_ref[1:2, :].astype(jnp.float32)
    ).astype(jnp.bfloat16)
    rows_ref[:, width:] = tail_ref[...]
    for way in (1, -1):
        for s in range(3):

            @pl.when(can_send(way, s))
            def _(way=way, s=s):
                hop(way, s).wait_send()

        for d in (1, 2, 3) if way > 0 else (0, 1, 2):

            @pl.when(passing(way, d))
            def _(way=way, d=d):
                onward(way, d).wait_send()


def attend(length, hidden, norm_gain, qk_gain, cosine, sine, tail, w_qkv, cache, w_out):
    span, cols = hidden.shape
    width = cols * 4
    rows = span // 4
    half = jnp.bfloat16
    vmem = pl.BlockSpec(memory_space=pltpu.VMEM)
    anywhere = pl.BlockSpec(memory_space=pl.ANY)
    dma = pltpu.SemaphoreType.DMA
    return pl.pallas_call(
        attend_kernel,
        out_shape=(
            jax.ShapeDtypeStruct((rows, width + TAIL), half),
            jax.ShapeDtypeStruct((rows, width), half),
            jax.ShapeDtypeStruct((2, span, cols), half),
        ),
        in_specs=[pl.BlockSpec(memory_space=pltpu.SMEM)] + [vmem] * 6 + [anywhere] * 3,
        out_specs=(vmem, vmem, vmem),
        scratch_shapes=[
            pltpu.VMEM((4, span, cols), half),
            pltpu.VMEM(w_qkv.shape, half),
            pltpu.VMEM(cache.shape, half),
            pltpu.VMEM(w_out.shape, half),
            pltpu.VMEM((3, span, cols), jnp.float32),
            pltpu.VMEM((span, 128), jnp.float32),
            pltpu.VMEM((span, cols), half),
            pltpu.VMEM((4, rows, width), jnp.float32),
            pltpu.VMEM((4, rows, width), half),
            pltpu.VMEM((4, rows, width), half),
            pltpu.VMEM((4, rows, width), half),
            pltpu.VMEM((4, rows, width), half),
            dma((3,)),
            dma((2, 3)),
            dma((2, 3)),
            pltpu.VMEM((8, span), jnp.float32),
            dma((4,)),
            pltpu.VMEM((4, 8, span), jnp.float32),
            dma((4,)),
            dma((2, 4)),
            dma((2, 4)),
        ],
        compiler_params=pltpu.CompilerParams(
            collective_id=2, has_side_effects=True, vmem_limit_bytes=VMEM_LIMIT
        ),
        name="attend",
    )(length, hidden, norm_gain, qk_gain, cosine, sine, tail, w_qkv, cache, w_out)


def layer_by_copies(
    hidden, norm_gain, w_qkv, qk_gain, w_out, cache, lengths, placing, routes, gate_w, w_gu, w_down
):
    position = lax.axis_index("wide")
    column = lax.axis_index("narrow")
    span = hidden.shape[1]
    rows, width = span // 4, hidden.shape[2] * 4
    held, _, _, inner = w_gu.shape
    length = jnp.sum(
        jnp.where(jnp.arange(lengths.shape[0], dtype=jnp.int32) == placing[position], lengths, 0)
    )
    positions = length.astype(jnp.float32) + jnp.arange(span, dtype=jnp.float32)
    frequency = 10000.0 ** (-(jnp.arange(HD // 2, dtype=jnp.float32) * (2.0 / HD)))
    angle = positions[:, None] * frequency[None, :]
    cosine, sine = jnp.cos(angle), jnp.sin(angle)
    table = router_table(
        lax.dynamic_slice_in_dim(routes[0], column * rows, rows, 0),
        lax.dynamic_slice_in_dim(gate_w[0], column * rows, rows, 0),
        held * 8,
    )
    filler = jnp.zeros((rows, TAIL - 24 * held), jnp.bfloat16)
    rows_in, after_rows, fresh = attend(
        length.reshape(1),
        hidden[0],
        norm_gain,
        qk_gain,
        jnp.concatenate([cosine, cosine], 1),
        jnp.concatenate([-sine, sine], 1),
        jnp.concatenate(in_three(table) + [filler], 1),
        jnp.transpose(w_qkv, (1, 0, 2)),
        cache[:, 0],
        w_out,
    )
    weighted = gather_experts(rows_in, w_gu.reshape(held, width, 2 * inner))
    result = reduce_experts(weighted, w_down.reshape(held * inner, width), after_rows)
    return result[None], fresh[:, None]


def experts_by_collectives(after_rows, gain, routes, gate_w, w_gu, w_down):
    position = lax.axis_index("wide")
    column = lax.axis_index("narrow")
    wide_size = lax.axis_size("wide")
    narrow = lax.axis_size("narrow")
    rows, full_width = after_rows.shape
    span_len, share_cols = rows * narrow, full_width // narrow
    after_all = lax.all_gather(after_rows, ("wide", "narrow"), axis=0, tiled=True)
    after_own = lax.dynamic_slice(
        after_all, (position * span_len, column * share_cols), (span_len, share_cols)
    )
    routed = normalize(after_all, gain).astype(jnp.bfloat16)
    held_experts = w_gu.shape[0]
    inner_cols = w_gu.shape[3]
    experts = held_experts * wide_size
    table = router_table(routes, gate_w, experts)
    table = lax.all_gather(table, "wide", axis=0, tiled=True)
    scale = lax.dynamic_slice_in_dim(table, position * held_experts, held_experts, 1)
    pieces = []
    for j in range(held_experts):
        gate_up = jnp.dot(
            routed,
            w_gu[j].reshape(full_width, 2 * inner_cols),
            preferred_element_type=jnp.float32,
        )
        activated = jax.nn.silu(gate_up[:, :inner_cols]) * gate_up[:, inner_cols:]
        pieces.append((activated * scale[:, j : j + 1]).astype(jnp.bfloat16))
    weighted = jnp.concatenate(pieces, 1)
    combined = jnp.dot(
        weighted,
        w_down.reshape(held_experts * inner_cols, full_width),
        preferred_element_type=jnp.float32,
    ).astype(jnp.bfloat16)
    combined = lax.psum_scatter(combined, "wide", scatter_dimension=0, tiled=True)
    expert_out = lax.psum_scatter(
        combined, "narrow", scatter_dimension=1, tiled=True
    ).astype(jnp.float32)
    return (after_own.astype(jnp.float32) + expert_out).astype(jnp.bfloat16)

def per_device(
    hidden, norm_gain, w_qkv, qk_gain, w_out, cache, lengths, placing, routes, gate_w, w_gu, w_down
):
    narrow = lax.axis_size("narrow")
    column = lax.axis_index("narrow")
    position = lax.axis_index("wide")
    span_len = hidden.shape[1]
    share_cols = hidden.shape[2]
    full_width = share_cols * narrow
    tokens = lax.all_gather(hidden[0], "narrow", axis=1, tiled=True)
    normed = normalize(tokens, norm_gain[0]).astype(jnp.bfloat16)
    local_cols = w_qkv.shape[2]
    projected = jnp.dot(
        normed, w_qkv.reshape(full_width, 3 * local_cols), preferred_element_type=jnp.float32
    )
    queries = projected[:, :local_cols]
    keys_new = projected[:, local_cols : 2 * local_cols]
    values_new = projected[:, 2 * local_cols :]
    squares = lax.psum((jnp.sum(queries * queries, -1), jnp.sum(keys_new * keys_new, -1)), "narrow")
    features = local_cols * narrow
    queries = queries * lax.rsqrt(squares[0][:, None] / features + 1e-05) * qk_gain[0]
    keys_new = keys_new * lax.rsqrt(squares[1][:, None] / features + 1e-05) * qk_gain[1]
    head_count = local_cols // HD
    length = lengths[placing[position]]
    positions = length.astype(jnp.float32) + jnp.arange(span_len, dtype=jnp.float32)
    queries = rotary(queries.reshape(span_len, head_count, HD), positions).astype(jnp.bfloat16)
    keys_new = rotary(keys_new.reshape(span_len, head_count, HD), positions).astype(jnp.bfloat16)
    values_new = values_new.reshape(span_len, head_count, HD).astype(jnp.bfloat16)
    stored = cache.shape[2]
    all_keys = jnp.concatenate([cache[0, 0].reshape(stored, head_count, HD), keys_new], 0)
    all_values = jnp.concatenate([cache[1, 0].reshape(stored, head_count, HD), values_new], 0)
    scores = jnp.einsum(
        "thd,jhd->htj", queries, all_keys, preferred_element_type=jnp.float32
    ) * HD ** (-0.5)
    key_index = jnp.arange(stored + span_len, dtype=jnp.int32)[None, :]
    query_index = jnp.arange(span_len, dtype=jnp.int32)[:, None]
    allowed = jnp.where(key_index < stored, key_index < length, key_index - stored <= query_index)
    scores = jnp.where(allowed[None], scores, -1e30)
    highest = jnp.max(scores, axis=-1, keepdims=True)
    exponent = jnp.exp(scores - highest)
    weights = exponent.astype(jnp.bfloat16)
    denominator = jnp.sum(exponent, axis=-1)
    summed = jnp.einsum("htj,jhd->thd", weights, all_values, preferred_element_type=jnp.float32)
    heads_out = (
        (summed / jnp.transpose(denominator)[:, :, None])
        .astype(jnp.bfloat16)
        .reshape(span_len, local_cols)
    )
    partial_out = jnp.dot(heads_out, w_out, preferred_element_type=jnp.float32)
    rows = span_len // narrow
    attention = lax.psum_scatter(
        partial_out.astype(jnp.bfloat16), "narrow", scatter_dimension=0, tiled=True
    ).astype(jnp.float32)
    own_rows = lax.dynamic_slice_in_dim(tokens, column * rows, rows, 0)
    after_rows = (own_rows.astype(jnp.float32) + attention).astype(jnp.bfloat16)
    result = experts_by_collectives(
        after_rows, norm_gain[1], routes[0], gate_w[0], w_gu, w_down
    )[None]
    fresh = jnp.stack(
        [keys_new.reshape(span_len, local_cols), values_new.reshape(span_len, local_cols)]
    )[:, None]
    return (result, fresh)


def solution(mesh):
    placed = (
        P("wide", None, "narrow"),
        P(),
        P(None, None, "narrow"),
        P(None, "narrow"),
        P("narrow", None),
        P(None, "wide", None, "narrow"),
        P(),
        P(),
        P("wide", None, None),
        P("wide", None, None),
        P("wide", None, None, "narrow"),
        P("wide", "narrow", None),
    )
    by_copies = mesh.shape["wide"] == 8 and mesh.shape["narrow"] == 4
    return jax.shard_map(
        layer_by_copies if by_copies else per_device,
        mesh=mesh,
        in_specs=placed,
        out_specs=(P("wide", None, "narrow"), P(None, "wide", None, "narrow")),
        check_vma=False,
    )
```
